32 devices in a mesh: seq: 8 (over z, x), head: 2 (over y), dp: 2 (over core).
Axes of the slice: x: 2, y: 2, z: 4, core: 2. Of those that a mesh axis runs over, the one named last changes fastest.
Arguments:
- queries: bfloat16 [2, 2048, 1024], P('dp', 'seq', 'head'), may hold values from -6 to 6
- key_rows: bfloat16 [2, 2048, 1024], P('dp', 'seq', 'head'), may hold values from -6 to 6
- value_rows: bfloat16 [2, 2048, 1024], P('dp', 'seq', 'head'), may hold values from -140 to 140
- stretch_doc: int32 [2, 8], P('dp', 'seq'), may hold values from 0 to 3, never falling along the last dimension, each value on 1 to 4 neighbouring positions
- head_gain: float32 [8, 128], P('head'), may hold values from 0.1 to 1.9
- w_out: bfloat16 [1024, 2048], P('head'), may hold values from -0.1875 to 0.1875
- cotangent: bfloat16 [2, 2048, 2048], P('dp', 'seq'), may hold values from -40 to 40
Outputs:
- layer_out: bfloat16 [2, 2048, 2048], P('dp', ('seq', 'head'))
- query_grad: bfloat16 [2, 2048, 1024], P('dp', 'seq', 'head')
- key_grad: bfloat16 [2, 2048, 1024], P('dp', 'seq', 'head')
- value_grad: bfloat16 [2, 2048, 1024], P('dp', 'seq', 'head')
- gain_grad: float32 [8, 128], P('head')
The draws below stay inside these ranges and needn't reach their ends.
Inputs may be any that keep to these rules, and one draw needn't show every extreme that they name: `stretch_doc`: document numbers never fall along a sequence; each document spans 1 to 4 whole stretches, and one spans exactly that many.
All inputs are finite; a program needn't handle non-finite values.
Results may differ from the reference program's by a relative error of at most 0.0055.
Values may be sent and summed in bfloat16 or wider, within the bound.
No kernel may reach another device: no remote copies, remote signals or barrier semaphores. Data moves between devices by JAX's collectives and lax.ppermute only.
A program may use at most 64 MiB of HBM per device.

```python
import math
import jax
import jax.numpy as jnp
import numpy as np
from jax import lax

D = 2048
HEADS = 8
DH = 128
STRETCH = 256
DOCS = 4
NCHUNK = 8
TOKENS = 2048
BATCH = 2
HD = 1024


def draw_value_rows(key, part):
    full_shape = (BATCH, TOKENS, HEADS * DH)
    col_key = jax.random.fold_in(key, 11)
    columns = jnp.exp(jax.random.uniform(col_key, (HEADS * DH,), jnp.float32, 0.0, math.log(10.0)))
    base_draw = jnp.clip(jax.random.normal(key, full_shape, jnp.float32), -6.0, 6.0)
    result = base_draw * columns
    return jnp.clip(result, -140.0, 140.0).astype(jnp.bfloat16)


def draw_cotangent(key, part):
    full_shape = (BATCH, TOKENS, D)
    position = jnp.arange(TOKENS, dtype=jnp.float32) / max(TOKENS - 1, 1)
    base_draw = jnp.clip(jax.random.normal(key, full_shape, jnp.float32), -6.0, 6.0)
    ramp_up = 1.0 + 2.0 * position
    result = base_draw * ramp_up[None, :, None]
    return jnp.clip(result, -40.0, 40.0).astype(jnp.bfloat16)


def block_scale(key, extent, cuts, smallest, top_value):
    loudness = 1.0
    for axis_at, blocks in cuts:
        heights = jax.random.uniform(jax.random.fold_in(jax.random.fold_in(key, 6), axis_at), (blocks,), jnp.float32, smallest / len(cuts), top_value / len(cuts))
        loudness = loudness * jnp.repeat(jnp.exp(heights), extent[axis_at] // blocks).reshape((-1,) + (1,) * (len(extent) - 1 - axis_at))
    return loudness


def length_profile(amount, total, limit, skew):
    weights = [(1 << 20) // math.isqrt(standing ** skew) + 1 for standing in range(2, amount + 1)]
    rest, given = total - limit - (amount - 1), [1] * (amount - 1)
    while rest > 0:
        free = [i for i in range(amount - 1) if given[i] < limit]
        pool, left = sum([weights[i] for i in free]), rest
        for i in free:
            addition = min(limit - given[i], max(1, left * weights[i] // pool), rest)
            given[i] = given[i] + addition
            rest = rest - addition
    return np.array([limit] + given)


def uneven(own_key, amount, total, most, skew):
    if amount == 2:
        one = jax.random.randint(own_key, (), max(1, total - most), min(most, total - 1) + 1)
        return jnp.stack([one, total - one])
    tallies = jnp.asarray(length_profile(amount, total, most, skew), jnp.int32)
    pairs = (amount - 1) // 2
    donor, sink = tallies[1:1 + 2 * pairs:2], tallies[2:2 + 2 * pairs:2]
    room = jnp.minimum(donor - 1, most - sink)
    shifted = jax.random.randint(jax.random.fold_in(own_key, 1), (pairs,), 0, 1 << 20) % (room + 1)
    tallies = tallies.at[1:1 + 2 * pairs:2].set(donor - shifted).at[2:2 + 2 * pairs:2].set(sink + shifted)
    return tallies[jax.random.permutation(jax.random.fold_in(own_key, 2), amount)]


def normal_values(key, extent, scale, reach, shards=(), kind=jnp.bfloat16):
    drawn = scale * jax.random.normal(key, extent, jnp.float32)
    if shards:
        drawn = drawn * block_scale(key, extent, shards, -0.22, 0.18)
    return jnp.clip(drawn, -reach, reach).astype(kind)


def setup_inputs(seed: int = 0) -> dict:
    splits = jax.random.split(jax.random.key(seed), 8)
    queries = normal_values(splits[0], (BATCH, TOKENS, HD), 1.0, 6.0, ((0, 2), (1, 8), (2, 2)))
    key_rows = normal_values(splits[1], (BATCH, TOKENS, HD), 1.0, 6.0, ((0, 2), (1, 8), (2, 2)))
    value_rows = draw_value_rows(jax.random.fold_in(splits[7], 71), 0)
    stretch_doc = jax.vmap(lambda own: jnp.searchsorted(jnp.cumsum(uneven(own, DOCS, NCHUNK, NCHUNK // 2, 2)), jnp.arange(NCHUNK), side="right"))(jax.random.split(splits[3], BATCH)).reshape((BATCH, NCHUNK)).astype(jnp.int32)
    head_gain = jnp.clip(1.0 + 0.18 * jax.random.normal(splits[4], (HEADS, DH), jnp.float32), 0.1, 1.9)
    w_out = normal_values(splits[5], (HD, D), HD ** -0.5, 0.1875, ((0, 2),))
    cotangent = draw_cotangent(jax.random.fold_in(splits[7], 71), 0)
    return dict(queries=queries, key_rows=key_rows, value_rows=value_rows, stretch_doc=stretch_doc, head_gain=head_gain, w_out=w_out, cotangent=cotangent)


epsilon = 1e-05
highest = lax.Precision.HIGHEST

def rounded(values_in):
    return lax.optimization_barrier(values_in.astype(jnp.bfloat16)).astype(jnp.float32)

def split_stretches(array_in):
    return array_in.reshape(BATCH, NCHUNK, STRETCH, HEADS, DH).transpose(1, 0, 3, 2, 4)

def join_stretches(array_in):
    return array_in.transpose(1, 0, 3, 2, 4).reshape(BATCH, TOKENS, HEADS * DH)

def reference(queries, key_rows, value_rows, stretch_doc, head_gain, w_out, cotangent):
    query_blk = split_stretches(queries)
    key_blk = split_stretches(key_rows)
    value_blk = split_stretches(value_rows)
    grad_blk = cotangent.reshape(BATCH, NCHUNK, STRETCH, D).transpose(1, 0, 2, 3)
    doc_ids = stretch_doc.T.astype(jnp.int32)
    causal = jnp.arange(STRETCH)[:, None] >= jnp.arange(STRETCH)[None, :]
    initial = (jnp.zeros((BATCH, HEADS, DH, DH), jnp.float32), jnp.full((BATCH,), -1, jnp.int32))

    def forward_step(carried_in, inputs):
        state_sum, last_doc = carried_in
        key_c, value_c, this_doc = inputs
        state_sum = jnp.where((this_doc == last_doc)[:, None, None, None], state_sum, jnp.zeros_like(state_sum))
        kv_sum = jnp.einsum('bhsd,bhse->bhde', key_c.astype(jnp.float32), value_c.astype(jnp.float32))
        return ((state_sum + kv_sum, this_doc), state_sum)
    _, states = lax.scan(forward_step, initial, (key_blk, value_blk, doc_ids))
    gain_b = head_gain.astype(jnp.float32)[None, :, None, :]

    def stretch_forward(inputs):
        query_c, key_c, value_c, state_c, grad_c = inputs
        query_f = query_c.astype(jnp.float32)
        scores = jnp.einsum('bhtd,bhsd->bhts', query_f, key_c.astype(jnp.float32))
        attn_weights = rounded(jnp.where(causal, scores, jnp.zeros_like(scores)))
        within = jnp.einsum('bhts,bhse->bhte', attn_weights, value_c.astype(jnp.float32))
        carried = jnp.einsum('bhtd,bhde->bhte', query_f, state_c, precision=highest)
        attended = within + carried
        inv_rms = lax.rsqrt(lax.optimization_barrier(jnp.mean(attended * attended, axis=-1, keepdims=True)) + epsilon)
        unit_rows = attended * inv_rms
        normed = (unit_rows * gain_b).astype(jnp.bfloat16)
        normed_rows = normed.transpose(0, 2, 1, 3).reshape(BATCH * STRETCH, HEADS * DH)
        layer_c = jnp.dot(normed_rows, w_out, preferred_element_type=jnp.float32).astype(jnp.bfloat16)
        grad_normed = jnp.dot(grad_c.reshape(BATCH * STRETCH, D), w_out.T, preferred_element_type=jnp.float32)
        grad_normed = grad_normed.reshape(BATCH, STRETCH, HEADS, DH).transpose(0, 2, 1, 3)
        gain_part = lax.optimization_barrier(jnp.sum(grad_normed * unit_rows, axis=(0, 2)))
        scaled = grad_normed * gain_b
        grad_attended = inv_rms * (scaled - unit_rows * lax.optimization_barrier(jnp.mean(scaled * unit_rows, axis=-1, keepdims=True)))
        grad_bf = grad_attended.astype(jnp.bfloat16)
        grad_f = lax.optimization_barrier(grad_bf).astype(jnp.float32)
        query_term = jnp.einsum('bhtd,bhte->bhde', query_f, grad_f)
        return (layer_c.reshape(BATCH, STRETCH, D), gain_part, grad_bf, query_term)
    layer_blk, gain_parts, grad_bfs, query_terms = lax.map(stretch_forward, (query_blk, key_blk, value_blk, states, grad_blk))

    def backward_step(carried_in, inputs):
        state_sum, last_doc = carried_in
        term_c, this_doc = inputs
        state_sum = jnp.where((this_doc == last_doc)[:, None, None, None], state_sum, jnp.zeros_like(state_sum))
        return ((state_sum + term_c, this_doc), state_sum)
    _, grad_states = lax.scan(backward_step, initial, (query_terms, doc_ids), reverse=True)

    def stretch_backward(inputs):
        query_c, key_c, value_c, state_c, grad_state_c, grad_bf = inputs
        query_f = query_c.astype(jnp.float32)
        key_f = key_c.astype(jnp.float32)
        value_f = value_c.astype(jnp.float32)
        grad_f = grad_bf.astype(jnp.float32)
        scores = jnp.einsum('bhtd,bhsd->bhts', query_f, key_f)
        attn_weights = rounded(jnp.where(causal, scores, jnp.zeros_like(scores)))
        grad_scores = jnp.einsum('bhte,bhse->bhts', grad_f, value_f)
        grad_weights = rounded(jnp.where(causal, grad_scores, jnp.zeros_like(grad_scores)))
        query_g = jnp.einsum('bhts,bhsd->bhtd', grad_weights, key_f) + jnp.einsum('bhte,bhde->bhtd', grad_f, state_c, precision=highest)
        key_g = jnp.einsum('bhts,bhtd->bhsd', grad_weights, query_f) + jnp.einsum('bhse,bhde->bhsd', value_f, grad_state_c, precision=highest)
        value_g = jnp.einsum('bhts,bhte->bhse', attn_weights, grad_f) + jnp.einsum('bhsd,bhde->bhse', key_f, grad_state_c, precision=highest)
        return (query_g.astype(jnp.bfloat16), key_g.astype(jnp.bfloat16), value_g.astype(jnp.bfloat16))
    query_gb, key_gb, value_gb = lax.map(stretch_backward, (query_blk, key_blk, value_blk, states, grad_states, grad_bfs))
    layer_out = layer_blk.transpose(1, 0, 2, 3).reshape(BATCH, TOKENS, D)
    gain_grad = lax.optimization_barrier(jnp.sum(gain_parts, axis=0)) / math.sqrt(BATCH * TOKENS)
    return (layer_out, join_stretches(query_gb), join_stretches(key_gb), join_stretches(value_gb), gain_grad)
```

```python
import functools
import math

import jax
import jax.numpy as jnp
from jax import lax
from jax.experimental import pallas as pl
from jax.experimental.pallas import tpu as pltpu
from jax.sharding import PartitionSpec as P

EPSILON = 1e-05
F32 = jnp.float32
BF16 = jnp.bfloat16
TAIL = 16


def nn(a, b):
    return lax.dot_general(a, b, (((1,), (0,)), ((), ())), preferred_element_type=F32)


def nt(a, b):
    return lax.dot_general(a, b, (((1,), (1,)), ((), ())), preferred_element_type=F32)


def tn(a, b):
    return lax.dot_general(a, b, (((0,), (0,)), ((), ())), preferred_element_type=F32)


def call(body, out_shapes, n_in, flops, moved, smem=()):
    spec = lambda i: pl.BlockSpec(memory_space=pltpu.SMEM if i in smem else pltpu.VMEM)
    return pl.pallas_call(
        body,
        out_shape=[jax.ShapeDtypeStruct(s, t) for s, t in out_shapes],
        in_specs=[spec(i) for i in range(n_in)],
        out_specs=[pl.BlockSpec(memory_space=pltpu.VMEM) for _ in out_shapes],
        cost_estimate=pl.CostEstimate(flops=flops, bytes_accessed=moved, transcendentals=0),
        compiler_params=pltpu.CompilerParams(vmem_limit_bytes=40 << 20),
    )


def swap_route(size, distance, odd):
    route = {i: i for i in range(size)}
    for i in range(size - distance):
        if (i // distance) % 2 == odd:
            route[i], route[i + distance] = i + distance, i
    return sorted(route.items())


def swaps(block, distance):
    size = lax.axis_size("seq")
    return [lax.ppermute(block, "seq", swap_route(size, distance, odd)) for odd in (0, 1)]


def exchange(block, axis, distance):
    size = lax.axis_size(axis)
    return lax.ppermute(block, axis, [(i, i ^ distance) for i in range(size)])


def put_doc(msg_ref, doc, rows):
    msg_ref[rows:, :] = jnp.full((TAIL, msg_ref.shape[1]), doc + 1, F32).astype(BF16)


def taken(even_ref, odd_ref, doc, distance, forward):
    rows = even_ref.shape[0] - TAIL
    me, size = lax.axis_index("seq"), lax.axis_size("seq")
    upper = lax.rem(lax.div(me, distance), 2)
    from_odd = upper == 0 if forward else upper == 1
    there = me >= distance if forward else me + distance < size
    got = jnp.where(from_odd, odd_ref[...].astype(F32), even_ref[...].astype(F32))
    mine = jnp.where(there, doc + 1, -1).astype(F32)
    return jnp.where(got[rows : rows + 1, :] == mine, got[:rows, :], 0.0)


def outer_body(heads, dim, doc_ref, key_ref, value_ref, sum_ref, msg_ref):
    for h in range(heads):
        cols, rows = slice(h * dim, (h + 1) * dim), slice(h * dim, (h + 1) * dim)
        total = tn(key_ref[:, cols], value_ref[:, cols])
        sum_ref[rows, :] = total
        msg_ref[rows, :] = total.astype(BF16)
    put_doc(msg_ref, doc_ref[0, 0], heads * dim)


def local_body(
    heads, dim, query_ref, key_ref, value_ref, cot_ref, w_ref, weight_ref, within_ref, normed_grad_ref
):
    tokens = query_ref.shape[0]
    causal = lax.broadcasted_iota(jnp.int32, (tokens, tokens), 0) >= lax.broadcasted_iota(
        jnp.int32, (tokens, tokens), 1
    )
    for h in range(heads):
        cols = slice(h * dim, (h + 1) * dim)
        scores = nt(query_ref[:, cols], key_ref[:, cols])
        weights = jnp.where(causal, scores, 0.0).astype(BF16)
        weight_ref[h * tokens : (h + 1) * tokens, :] = weights
        within_ref[:, cols] = nn(weights, value_ref[:, cols])
    normed_grad_ref[...] = nt(cot_ref[...], w_ref[...])


def merge_body(distance, forward, first, doc_ref, sum_ref, *refs):
    term_ref, refs = (None, refs) if first else (refs[0], refs[1:])
    even_ref, odd_ref, out_ref, msg_ref = refs
    rows = sum_ref.shape[0]
    doc = doc_ref[0, 0]
    term = taken(even_ref, odd_ref, doc, distance, forward)
    if not first:
        term = term + term_ref[...]
    out_ref[...] = term
    msg_ref[:rows, :] = (sum_ref[...] + term).astype(BF16)
    put_doc(msg_ref, doc, rows)


def forward_body(
    heads, dim, distance, doc_ref, query_ref, within_ref, normed_grad_ref, gain_ref, term_ref,
    even_ref, odd_ref, state_ref, keep_ref, send_ref, grad_ref, outer_ref, msg_ref, gain_grad_ref, normed_ref,
):
    doc = doc_ref[0, 0]
    half = keep_ref.shape[0]
    state_ref[...] = (
        term_ref[...] + taken(even_ref, odd_ref, doc, distance, True)
    ).astype(BF16)
    for h in range(heads):
        cols, rows = slice(h * dim, (h + 1) * dim), slice(h * dim, (h + 1) * dim)
        query = query_ref[:, cols]
        attended = within_ref[:, cols] + nn(query, state_ref[rows, :])
        inv_rms = lax.rsqrt(jnp.mean(attended * attended, axis=-1, keepdims=True) + EPSILON)
        unit = attended * inv_rms
        gain = gain_ref[h : h + 1, :]
        normed_ref[:, cols] = (unit * gain).astype(BF16)
        normed_grad = normed_grad_ref[:, cols]
        gain_grad_ref[h : h + 1, :] = jnp.sum(normed_grad * unit, axis=0, keepdims=True)
        scaled = normed_grad * gain
        grad = inv_rms * (scaled - unit * jnp.mean(scaled * unit, axis=-1, keepdims=True))
        grad = grad.astype(BF16)
        grad_ref[:, cols] = grad
        outer = tn(query, grad)
        outer_ref[rows, :] = outer
        msg_ref[rows, :] = outer.astype(BF16)
    put_doc(msg_ref, doc, heads * dim)
    head = lax.axis_index("head")
    keep_ref[...] = normed_ref[pl.ds(pl.multiple_of(head * half, half), half), :]
    send_ref[...] = normed_ref[pl.ds(pl.multiple_of((1 - head) * half, half), half), :]


def backward_body(
    heads, dim, query_ref, key_ref, value_ref, weight_ref, grad_ref, state_ref,
    query_grad_ref, key_part_ref, value_part_ref,
):
    tokens = query_ref.shape[0]
    causal = lax.broadcasted_iota(jnp.int32, (tokens, tokens), 0) >= lax.broadcasted_iota(
        jnp.int32, (tokens, tokens), 1
    )
    for h in range(heads):
        cols, rows = slice(h * dim, (h + 1) * dim), slice(h * dim, (h + 1) * dim)
        grad = grad_ref[:, cols]
        grad_scores = nt(grad, value_ref[:, cols])
        grad_weights = jnp.where(causal, grad_scores, 0.0).astype(BF16)
        query_grad_ref[:, cols] = (
            nn(grad_weights, key_ref[:, cols]) + nt(grad, state_ref[rows, :])
        ).astype(BF16)
        key_part_ref[:, cols] = tn(grad_weights, query_ref[:, cols])
        value_part_ref[:, cols] = tn(weight_ref[h * tokens : (h + 1) * tokens, :], grad)


def last_body(
    heads, dim, distance, doc_ref, key_ref, value_ref, key_part_ref, value_part_ref, term_ref,
    even_ref, odd_ref, key_grad_ref, value_grad_ref,
):
    state = (
        term_ref[...] + taken(even_ref, odd_ref, doc_ref[0, 0], distance, False)
    ).astype(BF16)
    for h in range(heads):
        cols, rows = slice(h * dim, (h + 1) * dim), slice(h * dim, (h + 1) * dim)
        key_grad_ref[:, cols] = (
            key_part_ref[:, cols] + nt(value_ref[:, cols], state[rows, :])
        ).astype(BF16)
        value_grad_ref[:, cols] = (
            value_part_ref[:, cols] + nn(key_ref[:, cols], state[rows, :])
        ).astype(BF16)


def layer_body(keep_ref, got_ref, own_ref, mine_ref, other_ref, out_ref):
    width = mine_ref.shape[0]
    core = lax.axis_index("dp")
    at = lambda i: pl.ds(pl.multiple_of(i * width, width), width)
    out_ref[...] = (
        nn(keep_ref[...], own_ref[...])
        + nn(got_ref[:, at(core)], mine_ref[...])
        + nn(got_ref[:, at(1 - core)], other_ref[...])
    ).astype(BF16)


def on_device(queries, key_rows, value_rows, stretch_doc, head_gain, w_out, cotangent):
    tokens, width = queries.shape[1:]
    heads, dim = head_gain.shape
    model = w_out.shape[1]
    size = lax.axis_size("seq")
    query, key, value, cot = queries[0], key_rows[0], value_rows[0], cotangent[0]
    matrix = 2 * tokens * dim * dim * heads
    square = 2 * tokens * tokens * dim * heads
    summed, message = (heads * dim, dim), (heads * dim + TAIL, dim)
    distances = [1]
    while 2 * distances[-1] - 1 < size // 2 - 1:
        distances.append(2 * distances[-1])

    core = lax.axis_index("dp")
    half = lax.dynamic_slice_in_dim(w_out, core * (width // 2), width // 2, 0)
    w_mine = exchange(half, "head", 1)
    w_other = exchange(w_mine, "dp", 1)

    def spread(outer, msg, forward):
        term = None
        for distance in distances[:-1]:
            first = term is None
            even, odd = swaps(msg, distance)
            term, msg = call(
                functools.partial(merge_body, distance, forward, first),
                [(summed, F32), (message, BF16)], 4 if first else 5, 0, 1 << 20, (0,),
            )(stretch_doc, outer, *(() if first else (term,)), even, odd)
        return term, *swaps(msg, distances[-1])

    outer, msg = call(
        functools.partial(outer_body, heads, dim), [(summed, F32), (message, BF16)], 3, matrix, 1 << 20, (0,)
    )(stretch_doc, key, value)
    weights, within, normed_grad = call(
        functools.partial(local_body, heads, dim),
        [((heads * tokens, tokens), BF16), ((tokens, width), F32), ((tokens, width), F32)],
        5, 2 * square + 2 * tokens * width * model, 6 << 20,
    )(query, key, value, cot, w_out)
    term, even, odd = spread(outer, msg, True)
    state, keep, send, grad, outer, msg, gain_part = pl.pallas_call(
        functools.partial(forward_body, heads, dim, distances[-1]),
        out_shape=[
            jax.ShapeDtypeStruct(s, t)
            for s, t in (
                (summed, BF16), ((tokens // 2, width), BF16), ((tokens // 2, width), BF16),
                ((tokens, width), BF16), (summed, F32), (message, BF16), ((heads, dim), F32),
            )
        ],
        in_specs=[pl.BlockSpec(memory_space=pltpu.SMEM)] + [pl.BlockSpec(memory_space=pltpu.VMEM)] * 7,
        out_specs=[pl.BlockSpec(memory_space=pltpu.VMEM)] * 7,
        scratch_shapes=[pltpu.VMEM((tokens, width), BF16)],
        cost_estimate=pl.CostEstimate(flops=2 * matrix, bytes_accessed=4 << 20, transcendentals=0),
        compiler_params=pltpu.CompilerParams(vmem_limit_bytes=40 << 20),
    )(stretch_doc, query, within, normed_grad, head_gain, term, even, odd)
    got = exchange(send, "head", 1)
    query_grad, key_part, value_part = call(
        functools.partial(backward_body, heads, dim),
        [((tokens, width), BF16), ((tokens, width), F32), ((tokens, width), F32)],
        6, 4 * square + matrix, 4 << 20,
    )(query, key, value, weights, grad, state)
    if size & (size - 1) == 0:
        gain_sum = gain_part
        for axis, distance in [("dp", 1)] + [("seq", 1 << i) for i in range(size.bit_length() - 1)]:
            gain_sum = gain_sum + exchange(gain_sum, axis, distance)
    else:
        gain_sum = lax.psum(gain_part, ("seq", "dp"))
    gain_grad = gain_sum / math.sqrt(size * lax.axis_size("dp") * tokens)
    term, even, odd = spread(outer, msg, False)
    key_grad, value_grad = call(
        functools.partial(last_body, heads, dim, distances[-1]),
        [((tokens, width), BF16), ((tokens, width), BF16)], 8, 2 * matrix, 3 << 20, (0,),
    )(stretch_doc, key, value, key_part, value_part, term, even, odd)
    (layer_out,) = call(
        layer_body, [((tokens // 2, model), BF16)], 5, 2 * tokens * width * model, 6 << 20
    )(keep, got, w_out, w_mine, w_other)
    return layer_out[None], query_grad[None], key_grad[None], value_grad[None], gain_grad


def solution(mesh):
    rows = P("dp", "seq", "head")
    return jax.shard_map(
        on_device,
        mesh=mesh,
        in_specs=(rows, rows, rows, P("dp", "seq"), P("head", None), P("head", None), P("dp", "seq", None)),
        out_specs=(P("dp", ("seq", "head"), None), rows, rows, rows, P("head", None)),
        check_vma=False,
    )
```

```python
import functools
import math

import jax
import jax.numpy as jnp
from jax import lax
from jax.experimental import pallas as pl
from jax.experimental.pallas import tpu as pltpu
from jax.sharding import PartitionSpec as P

EPSILON = 1e-05
F32 = jnp.float32
BF16 = jnp.bfloat16
TAIL = 16
GAIN = 4


def nn(a, b):
    return lax.dot_general(a, b, (((1,), (0,)), ((), ())), preferred_element_type=F32)


def nt(a, b):
    return lax.dot_general(a, b, (((1,), (1,)), ((), ())), preferred_element_type=F32)


def tn(a, b):
    return lax.dot_general(a, b, (((0,), (0,)), ((), ())), preferred_element_type=F32)


def call(body, outs, places, flops, moved, scratch=()):
    space = {"s": pltpu.SMEM, "v": pltpu.VMEM, "h": pltpu.HBM}
    return pl.pallas_call(
        body,
        out_shape=[jax.ShapeDtypeStruct(s, t) for s, t in outs],
        in_specs=[pl.BlockSpec(memory_space=space[p]) for p in places],
        out_specs=[pl.BlockSpec(memory_space=pltpu.VMEM) for _ in outs],
        scratch_shapes=list(scratch),
        cost_estimate=pl.CostEstimate(flops=flops, bytes_accessed=moved, transcendentals=0),
        compiler_params=pltpu.CompilerParams(vmem_limit_bytes=40 << 20),
    )


def swap_route(size, distance, odd):
    route = {i: i for i in range(size)}
    for i in range(size - distance):
        if (i // distance) % 2 == odd:
            route[i], route[i + distance] = i + distance, i
    return sorted(route.items())


def swaps(block, distance):
    size = lax.axis_size("seq")
    return [lax.ppermute(block, "seq", swap_route(size, distance, odd)) for odd in (0, 1)]


def exchange(block, axis, distance):
    size = lax.axis_size(axis)
    return lax.ppermute(block, axis, [(i, i ^ distance) for i in range(size)])


def put_tail(msg_ref, doc, gain=None):
    rows, dim = msg_ref.shape[0] - TAIL, msg_ref.shape[1]
    high = jnp.zeros((GAIN, dim), F32) if gain is None else gain.astype(BF16).astype(F32)
    low = jnp.zeros((GAIN, dim), F32) if gain is None else gain - high
    low = low.astype(BF16).astype(F32)
    number = jnp.full((TAIL - 2 * GAIN, dim), doc + 1, jnp.int32).astype(F32)
    msg_ref[rows:, :] = jnp.concatenate([high, low, number], axis=0).astype(BF16)
    return high + low


def sent_gain(msg_ref):
    tail = msg_ref[msg_ref.shape[0] - TAIL :, :].astype(F32)
    return tail[:GAIN, :] + tail[GAIN : 2 * GAIN, :]


def taken(even_ref, odd_ref, doc, distance, forward):
    rows = even_ref.shape[0] - TAIL
    me, size = lax.axis_index("seq"), lax.axis_size("seq")
    upper = lax.rem(lax.div(me, distance), 2)
    from_odd = upper == 0 if forward else upper == 1
    there = me >= distance if forward else me + distance < size
    got = jnp.where(from_odd, odd_ref[...].astype(F32), even_ref[...].astype(F32))
    mine = jnp.where(there, doc + 1, -1).astype(F32)
    number = got[rows + 2 * GAIN : rows + 2 * GAIN + 1, :]
    return jnp.where(number == mine, got[:rows, :], 0.0)


def opening_body(
    heads, dim, doc_ref, query_hbm, key_hbm, value_hbm, w_hbm,
    query_ref, key_ref, value_ref, half_ref, sum_ref, msg_ref, sems,
):
    width = half_ref.shape[0]
    core = lax.axis_index("dp")
    ours = w_hbm.at[pl.ds(pl.multiple_of(core * width, width), width), :]
    copies = [
        pltpu.make_async_copy(src, dst, sems.at[i])
        for i, (src, dst) in enumerate(
            ((key_hbm, key_ref), (value_hbm, value_ref), (ours, half_ref), (query_hbm, query_ref))
        )
    ]
    for copy in copies:
        copy.start()
    put_tail(msg_ref, doc_ref[0, 0])
    copies[0].wait()
    copies[1].wait()
    for h in range(heads):
        cols, rows = slice(h * dim, (h + 1) * dim), slice(h * dim, (h + 1) * dim)
        total = tn(key_ref[:, cols], value_ref[:, cols])
        sum_ref[rows, :] = total
        msg_ref[rows, :] = total.astype(BF16)
    copies[2].wait()
    copies[3].wait()


def local_body(
    heads, dim, query_ref, key_ref, value_ref, cot_hbm, w_ref,
    weight_ref, within_ref, normed_grad_ref, cot_ref, sem,
):
    copy = pltpu.make_async_copy(cot_hbm, cot_ref, sem)
    copy.start()
    tokens = query_ref.shape[0]
    causal = lax.broadcasted_iota(jnp.int32, (tokens, tokens), 0) >= lax.broadcasted_iota(
        jnp.int32, (tokens, tokens), 1
    )
    for h in range(heads):
        cols = slice(h * dim, (h + 1) * dim)
        scores = nt(query_ref[:, cols], key_ref[:, cols])
        weights = jnp.where(causal, scores, 0.0).astype(BF16)
        weight_ref[h * tokens : (h + 1) * tokens, :] = weights
        within_ref[:, cols] = nn(weights, value_ref[:, cols])
    copy.wait()
    normed_grad_ref[...] = nt(cot_ref[...], w_ref[...])


def merge_body(distance, forward, first, gains, doc_ref, sum_ref, *refs):
    term_ref, refs = (None, refs) if first else (refs[0], refs[1:])
    even_ref, odd_ref, own_ref, out_ref, msg_ref = refs[:5]
    rows = sum_ref.shape[0]
    doc = doc_ref[0, 0]
    term = taken(even_ref, odd_ref, doc, distance, forward)
    if not first:
        term = term + term_ref[...]
    out_ref[...] = term
    msg_ref[:rows, :] = (sum_ref[...] + term).astype(BF16)
    if gains:
        gain = sent_gain(own_ref) + sent_gain(even_ref)
        refs[5][...] = put_tail(msg_ref, doc, gain)
    else:
        put_tail(msg_ref, doc)


def forward_body(
    heads, dim, distance, doc_ref, query_ref, within_ref, normed_grad_ref, gain_ref, term_ref,
    even_ref, odd_ref, state_ref, keep_ref, send_ref, grad_ref, outer_ref, msg_ref, gain_grad_ref, normed_ref,
):
    doc = doc_ref[0, 0]
    half = keep_ref.shape[0]
    state_ref[...] = (
        term_ref[...] + taken(even_ref, odd_ref, doc, distance, True)
    ).astype(BF16)
    for h in range(heads):
        cols, rows = slice(h * dim, (h + 1) * dim), slice(h * dim, (h + 1) * dim)
        query = query_ref[:, cols]
        attended = within_ref[:, cols] + nn(query, state_ref[rows, :])
        inv_rms = lax.rsqrt(jnp.mean(attended * attended, axis=-1, keepdims=True) + EPSILON)
        unit = attended * inv_rms
        gain = gain_ref[h : h + 1, :]
        normed_ref[:, cols] = (unit * gain).astype(BF16)
        normed_grad = normed_grad_ref[:, cols]
        gain_grad_ref[h : h + 1, :] = jnp.sum(normed_grad * unit, axis=0, keepdims=True)
        scaled = normed_grad * gain
        grad = inv_rms * (scaled - unit * jnp.mean(scaled * unit, axis=-1, keepdims=True))
        grad = grad.astype(BF16)
        grad_ref[:, cols] = grad
        outer = tn(query, grad)
        outer_ref[rows, :] = outer
        msg_ref[rows, :] = outer.astype(BF16)
    put_tail(msg_ref, doc, gain_grad_ref[...])
    head = lax.axis_index("head")
    keep_ref[...] = normed_ref[pl.ds(pl.multiple_of(head * half, half), half), :]
    send_ref[...] = normed_ref[pl.ds(pl.multiple_of((1 - head) * half, half), half), :]


def backward_body(
    heads, dim, query_ref, key_ref, value_ref, weight_ref, grad_ref, state_ref,
    query_grad_ref, key_part_ref, value_part_ref,
):
    tokens = query_ref.shape[0]
    causal = lax.broadcasted_iota(jnp.int32, (tokens, tokens), 0) >= lax.broadcasted_iota(
        jnp.int32, (tokens, tokens), 1
    )
    for h in range(heads):
        cols, rows = slice(h * dim, (h + 1) * dim), slice(h * dim, (h + 1) * dim)
        grad = grad_ref[:, cols]
        grad_scores = nt(grad, value_ref[:, cols])
        grad_weights = jnp.where(causal, grad_scores, 0.0).astype(BF16)
        query_grad_ref[:, cols] = (
            nn(grad_weights, key_ref[:, cols]) + nt(grad, state_ref[rows, :])
        ).astype(BF16)
        key_part_ref[:, cols] = tn(grad_weights, query_ref[:, cols])
        value_part_ref[:, cols] = tn(weight_ref[h * tokens : (h + 1) * tokens, :], grad)


def last_body(
    heads, dim, distance, gains, doc_ref, key_ref, value_ref, key_part_ref, value_part_ref, term_ref,
    even_ref, odd_ref, *refs,
):
    if gains:
        own_ref, far_ref, farther_ref, key_grad_ref, value_grad_ref, gain_ref = refs
        near = sent_gain(own_ref) + sent_gain(even_ref)
        gain_ref[...] = near + (far_ref[...] + farther_ref[...])
    else:
        key_grad_ref, value_grad_ref = refs
    state = (
        term_ref[...] + taken(even_ref, odd_ref, doc_ref[0, 0], distance, False)
    ).astype(BF16)
    for h in range(heads):
        cols, rows = slice(h * dim, (h + 1) * dim), slice(h * dim, (h + 1) * dim)
        key_grad_ref[:, cols] = (
            key_part_ref[:, cols] + nt(value_ref[:, cols], state[rows, :])
        ).astype(BF16)
        value_grad_ref[:, cols] = (
            value_part_ref[:, cols] + nn(key_ref[:, cols], state[rows, :])
        ).astype(BF16)


def layer_body(keep_ref, got_ref, own_ref, mine_ref, other_ref, out_ref):
    width = mine_ref.shape[0]
    core = lax.axis_index("dp")
    at = lambda i: pl.ds(pl.multiple_of(i * width, width), width)
    out_ref[...] = (
        nn(keep_ref[...], own_ref[...])
        + nn(got_ref[:, at(core)], mine_ref[...])
        + nn(got_ref[:, at(1 - core)], other_ref[...])
    ).astype(BF16)


def on_device(queries, key_rows, value_rows, stretch_doc, head_gain, w_out, cotangent):
    tokens, width = queries.shape[1:]
    heads, dim = head_gain.shape
    model = w_out.shape[1]
    size = lax.axis_size("seq")
    matrix = 2 * tokens * dim * dim * heads
    square = 2 * tokens * tokens * dim * heads
    rows, summed, message = (tokens, width), (heads * dim, dim), (heads * dim + TAIL, dim)
    small = (heads, dim)
    distances = [1]
    while 2 * distances[-1] - 1 < size // 2 - 1:
        distances.append(2 * distances[-1])
    last = distances[-1]
    gains = size & (size - 1) == 0 and len(distances) > 1

    def spread(outer, msg, forward):
        term, gain = None, None
        for distance in distances[:-1]:
            first = term is None
            carry = gains and not forward
            even, odd = swaps(msg, distance)
            term, msg, *gain = call(
                functools.partial(merge_body, distance, forward, first, carry),
                [(summed, F32), (message, BF16)] + [(small, F32)] * carry,
                "s" + "v" * (4 if first else 5), flops=0, moved=1 << 20,
            )(stretch_doc, outer, *(() if first else (term,)), even, odd, msg)
        return term, *swaps(msg, last), msg, gain

    in_hbm = lambda block: pltpu.with_memory_space_constraint(block, pltpu.HBM)
    query, key, value, half, outer, msg = call(
        functools.partial(opening_body, heads, dim),
        [(rows, BF16)] * 3 + [((width // 2, model), BF16), (summed, F32), (message, BF16)],
        "shhhh", flops=matrix, moved=4 << 20, scratch=[pltpu.SemaphoreType.DMA((4,))],
    )(stretch_doc, in_hbm(queries[0]), in_hbm(key_rows[0]), in_hbm(value_rows[0]), in_hbm(w_out))
    w_mine = exchange(half, "head", 1)
    weights, within, normed_grad = call(
        functools.partial(local_body, heads, dim),
        [((heads * tokens, tokens), BF16), (rows, F32), (rows, F32)],
        "vvvhv", flops=2 * square + 2 * tokens * width * model, moved=6 << 20,
        scratch=[pltpu.VMEM((tokens, model), BF16), pltpu.SemaphoreType.DMA],
    )(query, key, value, in_hbm(cotangent[0]), w_out)
    term, even, odd, _, _ = spread(outer, msg, True)
    state, keep, send, grad, outer, msg, gain_part = call(
        functools.partial(forward_body, heads, dim, last),
        [
            (summed, BF16), ((tokens // 2, width), BF16), ((tokens // 2, width), BF16),
            (rows, BF16), (summed, F32), (message, BF16), (small, F32),
        ],
        "svvvvvvv", flops=2 * matrix, moved=4 << 20, scratch=[pltpu.VMEM(rows, BF16)],
    )(stretch_doc, query, within, normed_grad, head_gain, term, even, odd)
    got = exchange(send, "head", 1)
    query_grad, key_part, value_part = call(
        functools.partial(backward_body, heads, dim),
        [(rows, BF16), (rows, F32), (rows, F32)],
        "vvvvvv", flops=4 * square + matrix, moved=4 << 20,
    )(query, key, value, weights, grad, state)
    term, even, odd, msg, gain = spread(outer, msg, False)
    even, got = lax.optimization_barrier((even, got))
    far = []
    if gains:
        far = [msg] + [exchange(gain[0], "seq", d) for d in (size // 2, size // 2 + last)]
    key_grad, value_grad, *gain = call(
        functools.partial(last_body, heads, dim, last, gains),
        [(rows, BF16), (rows, BF16)] + [(small, F32)] * gains,
        "s" + "v" * (7 + len(far)), flops=2 * matrix, moved=3 << 20,
    )(stretch_doc, key, value, key_part, value_part, term, even, odd, *far)
    if gains:
        gain[0], w_mine = lax.optimization_barrier((gain[0], w_mine))
        gain_sum = gain[0] + exchange(gain[0], "dp", 1)
    else:
        gain_sum = lax.psum(gain_part, ("seq", "dp"))
    gain_grad = gain_sum / math.sqrt(size * lax.axis_size("dp") * tokens)
    w_other = exchange(w_mine, "dp", 1)
    (layer_out,) = call(
        layer_body, [((tokens // 2, model), BF16)], "vvvvv", flops=2 * tokens * width * model, moved=6 << 20
    )(keep, got, w_out, w_mine, w_other)
    return layer_out[None], query_grad[None], key_grad[None], value_grad[None], gain_grad


def solution(mesh):
    rows = P("dp", "seq", "head")
    return jax.shard_map(
        on_device,
        mesh=mesh,
        in_specs=(rows, rows, rows, P("dp", "seq"), P("head", None), P("head", None), P("dp", "seq", None)),
        out_specs=(P("dp", ("seq", "head"), None), rows, rows, rows, P("head", None)),
        check_vma=False,
    )
```

```python
import functools
import math

import jax
import jax.numpy as jnp
from jax import lax
from jax.experimental import pallas as pl
from jax.experimental.pallas import tpu as pltpu
from jax.sharding import PartitionSpec as P

EPSILON = 1e-05
F32 = jnp.float32
BF16 = jnp.bfloat16
TAIL = 16
GAIN = 4


def nn(a, b):
    return lax.dot_general(a, b, (((1,), (0,)), ((), ())), preferred_element_type=F32)


def nt(a, b):
    return lax.dot_general(a, b, (((1,), (1,)), ((), ())), preferred_element_type=F32)


def tn(a, b):
    return lax.dot_general(a, b, (((0,), (0,)), ((), ())), preferred_element_type=F32)


def call(body, outs, places, flops, moved, scratch=()):
    space = {"s": pltpu.SMEM, "v": pltpu.VMEM, "h": pltpu.HBM}
    return pl.pallas_call(
        body,
        out_shape=[jax.ShapeDtypeStruct(s, t) for s, t in outs],
        in_specs=[pl.BlockSpec(memory_space=space[p]) for p in places],
        out_specs=[pl.BlockSpec(memory_space=pltpu.VMEM) for _ in outs],
        scratch_shapes=list(scratch),
        cost_estimate=pl.CostEstimate(flops=flops, bytes_accessed=moved, transcendentals=0),
        compiler_params=pltpu.CompilerParams(vmem_limit_bytes=40 << 20),
    )


def pairing(size, pairs):
    partner = {i: (j, False) for a, b in pairs for i, j in ((a, b), (b, a))}
    route = []
    for i in range(size):
        to, same_stretch = partner.get(i, (i, True))
        route += [(2 * i + core, 2 * to + (core ^ same_stretch)) for core in (0, 1)]
    return route


def exchange(block, pairs):
    return lax.ppermute(block, ("seq", "dp"), pairing(lax.axis_size("seq"), pairs))


def blocks(size, distance, odd):
    return [(i, i + distance) for i in range(size - distance) if (i // distance) % 2 == odd]


def swaps(block, distance):
    size = lax.axis_size("seq")
    return [exchange(block, blocks(size, distance, odd)) for odd in (0, 1)]


def flipped(block, distance, cores):
    route = [
        (2 * i + core, 2 * (i ^ distance) + (core ^ cores))
        for i in range(lax.axis_size("seq"))
        for core in (0, 1)
    ]
    return lax.ppermute(block, ("seq", "dp"), route)


def put_tail(msg_ref, number, gain=None):
    rows, dim = msg_ref.shape[0] - TAIL, msg_ref.shape[1]
    high = jnp.zeros((GAIN, dim), F32) if gain is None else gain.astype(BF16).astype(F32)
    low = jnp.zeros((GAIN, dim), F32) if gain is None else gain - high
    low = low.astype(BF16).astype(F32)
    number = jnp.broadcast_to(number, (TAIL - 2 * GAIN, dim))
    msg_ref[rows:, :] = jnp.concatenate([high, low, number], axis=0).astype(BF16)
    return high + low


def sent_gain(msg_ref):
    tail = msg_ref[msg_ref.shape[0] - TAIL :, :].astype(F32)
    return tail[:GAIN, :] + tail[GAIN : 2 * GAIN, :]


def opened(msg):
    msg = msg.astype(F32)
    rows = msg.shape[0] - TAIL
    return msg[:rows, :], msg[rows + 2 * GAIN : rows + 2 * GAIN + 1, :]


def taken(even_ref, odd_ref, number, distance, forward):
    me, size = lax.axis_index("seq"), lax.axis_size("seq")
    upper = lax.rem(lax.div(me, distance), 2)
    from_odd = upper == 0 if forward else upper == 1
    there = me >= distance if forward else me + distance < size
    sums, theirs = opened(jnp.where(from_odd, odd_ref[...], even_ref[...]))
    return jnp.where(theirs == jnp.where(there, number, -1.0), sums, 0.0)


def beside(pair_ref, far_ref, number, forward):
    me, size = lax.axis_index("seq"), lax.axis_size("seq")
    in_pair = lax.rem(me, 2) == (1 if forward else 0)
    there = in_pair | (me >= 3 if forward else me + 3 < size)
    sums, theirs = opened(jnp.where(in_pair, pair_ref[...], far_ref[...]))
    return jnp.where(theirs == jnp.where(there, number, -1.0), sums, 0.0)


def total(refs, number, distance, forward):
    *near, even_ref, odd_ref = refs
    if len(near) == 1:
        first = near[0][...]
    else:
        first = beside(*near, number, forward)
    return first + taken(even_ref, odd_ref, number, distance, forward)


def opening_body(
    heads, dim, doc_ref, query_hbm, key_hbm, value_hbm, w_hbm,
    query_ref, key_ref, value_ref, w_ref, number_ref, sum_ref, msg_ref, sems,
):
    copies = [
        pltpu.make_async_copy(src, dst, sems.at[i])
        for i, (src, dst) in enumerate(
            ((key_hbm, key_ref), (value_hbm, value_ref), (query_hbm, query_ref), (w_hbm, w_ref))
        )
    ]
    for copy in copies:
        copy.start()
    number = jnp.broadcast_to(doc_ref[...].astype(F32) + 1.0, number_ref.shape)
    number_ref[...] = number
    put_tail(msg_ref, number[:1, :])
    copies[0].wait()
    copies[1].wait()
    for h in range(heads):
        cols, rows = slice(h * dim, (h + 1) * dim), slice(h * dim, (h + 1) * dim)
        sums = tn(key_ref[:, cols], value_ref[:, cols])
        sum_ref[rows, :] = sums
        msg_ref[rows, :] = sums.astype(BF16)
    copies[2].wait()
    copies[3].wait()


def local_body(
    heads, dim, query_ref, key_ref, value_ref, cot_hbm, w_ref,
    weight_ref, within_ref, normed_grad_ref, cot_ref, sem,
):
    copy = pltpu.make_async_copy(cot_hbm, cot_ref, sem)
    copy.start()
    tokens = query_ref.shape[0]
    causal = lax.broadcasted_iota(jnp.int32, (tokens, tokens), 0) >= lax.broadcasted_iota(
        jnp.int32, (tokens, tokens), 1
    )
    for h in range(heads):
        cols = slice(h * dim, (h + 1) * dim)
        scores = nt(query_ref[:, cols], key_ref[:, cols])
        weights = jnp.where(causal, scores, 0.0).astype(BF16)
        weight_ref[h * tokens : (h + 1) * tokens, :] = weights
        within_ref[:, cols] = nn(weights, value_ref[:, cols])
    copy.wait()
    normed_grad_ref[...] = nt(cot_ref[...], w_ref[...])


def merge_gain(gains, own_ref, other_ref):
    return sent_gain(own_ref) + sent_gain(other_ref) if gains else None


def pair_body(forward, gains, number_ref, sum_ref, own_ref, pair_ref, msg_ref):
    rows = sum_ref.shape[0]
    number = number_ref[:1, :]
    leads = lax.rem(lax.axis_index("seq"), 2) == (1 if forward else 0)
    sums, theirs = opened(pair_ref[...])
    mine = sum_ref[...]
    same = theirs == number
    keep_mine, keep_theirs = same | leads, same | jnp.logical_not(leads)
    msg_ref[:rows, :] = (jnp.where(keep_mine, mine, 0.0) + jnp.where(keep_theirs, sums, 0.0)).astype(BF16)
    put_tail(msg_ref, jnp.where(leads, number, theirs), merge_gain(gains, own_ref, pair_ref))


def merge_body(distance, forward, gains, number_ref, sum_ref, own_ref, *refs):
    *term_ref, even_ref, odd_ref, out_ref, msg_ref = refs
    rows = sum_ref.shape[0]
    number = number_ref[:1, :]
    term = taken(even_ref, odd_ref, number, distance, forward)
    if term_ref:
        term = term + term_ref[0][...]
    out_ref[...] = term
    msg_ref[:rows, :] = (sum_ref[...] + term).astype(BF16)
    put_tail(msg_ref, number, merge_gain(gains, own_ref, even_ref))


def gain_body(own_ref, other_ref, out_ref):
    out_ref[...] = merge_gain(True, own_ref, other_ref)


def forward_body(
    heads, dim, distance, number_ref, query_ref, within_ref, normed_grad_ref, gain_ref, w_ref, *refs
):
    *sum_refs, state_ref, keep_ref, send_ref, grad_ref, outer_ref, msg_ref, gain_grad_ref, normed_ref = refs
    half = keep_ref.shape[0]
    number = number_ref[:1, :]
    state_ref[...] = total(sum_refs, number, distance, True).astype(BF16)
    for h in range(heads):
        cols, rows = slice(h * dim, (h + 1) * dim), slice(h * dim, (h + 1) * dim)
        query = query_ref[:, cols]
        attended = within_ref[:, cols] + nn(query, state_ref[rows, :])
        inv_rms = lax.rsqrt(jnp.mean(attended * attended, axis=-1, keepdims=True) + EPSILON)
        unit = attended * inv_rms
        gain = gain_ref[h : h + 1, :]
        normed_ref[:, cols] = (unit * gain).astype(BF16)
        normed_grad = normed_grad_ref[:, cols]
        gain_grad_ref[h : h + 1, :] = jnp.sum(normed_grad * unit, axis=0, keepdims=True)
        scaled = normed_grad * gain
        grad = inv_rms * (scaled - unit * jnp.mean(scaled * unit, axis=-1, keepdims=True))
        grad = grad.astype(BF16)
        grad_ref[:, cols] = grad
        outer = tn(query, grad)
        outer_ref[rows, :] = outer
        msg_ref[rows, :] = outer.astype(BF16)
    put_tail(msg_ref, number, gain_grad_ref[...])
    head = lax.axis_index("head")
    keep_ref[...] = normed_ref[pl.ds(pl.multiple_of(head * half, half), half), :]
    send_ref[...] = nn(
        normed_ref[pl.ds(pl.multiple_of((1 - head) * half, half), half), :], w_ref[...]
    ).astype(BF16)


def backward_body(
    heads, dim, query_ref, key_ref, value_ref, weight_ref, grad_ref, state_ref,
    query_grad_ref, key_part_ref, value_part_ref,
):
    tokens = query_ref.shape[0]
    causal = lax.broadcasted_iota(jnp.int32, (tokens, tokens), 0) >= lax.broadcasted_iota(
        jnp.int32, (tokens, tokens), 1
    )
    for h in range(heads):
        cols, rows = slice(h * dim, (h + 1) * dim), slice(h * dim, (h + 1) * dim)
        grad = grad_ref[:, cols]
        grad_scores = nt(grad, value_ref[:, cols])
        grad_weights = jnp.where(causal, grad_scores, 0.0).astype(BF16)
        query_grad_ref[:, cols] = (
            nn(grad_weights, key_ref[:, cols]) + nt(grad, state_ref[rows, :])
        ).astype(BF16)
        key_part_ref[:, cols] = tn(grad_weights, query_ref[:, cols])
        value_part_ref[:, cols] = tn(weight_ref[h * tokens : (h + 1) * tokens, :], grad)


def last_body(
    heads, dim, distance, number_ref, key_ref, value_ref, key_part_ref, value_part_ref, *refs
):
    *sum_refs, key_grad_ref, value_grad_ref = refs
    state = total(sum_refs, number_ref[:1, :], distance, False).astype(BF16)
    for h in range(heads):
        cols, rows = slice(h * dim, (h + 1) * dim), slice(h * dim, (h + 1) * dim)
        key_grad_ref[:, cols] = (
            key_part_ref[:, cols] + nt(value_ref[:, cols], state[rows, :])
        ).astype(BF16)
        value_grad_ref[:, cols] = (
            value_part_ref[:, cols] + nn(key_ref[:, cols], state[rows, :])
        ).astype(BF16)


def layer_body(scale, keep_ref, w_ref, got_ref, *refs):
    *gain_refs, out_ref, gain_grad_ref = refs
    out_ref[...] = (nn(keep_ref[...], w_ref[...]) + got_ref[...].astype(F32)).astype(BF16)
    parts = [ref[...] for ref in gain_refs]
    if len(parts) == 4:
        parts = [(parts[0] + parts[1]) + (parts[2] + parts[3])]
    gain_grad_ref[...] = parts[0] * scale


def on_device(queries, key_rows, value_rows, stretch_doc, head_gain, w_out, cotangent):
    tokens, width = queries.shape[1:]
    heads, dim = head_gain.shape
    model = w_out.shape[1]
    size = lax.axis_size("seq")
    matrix = 2 * tokens * dim * dim * heads
    square = 2 * tokens * tokens * dim * heads
    layer = tokens * width * model
    rows, summed, message = (tokens, width), (heads * dim, dim), (heads * dim + TAIL, dim)
    small, half = (heads, dim), (tokens // 2, model)
    distances = [1]
    while 2 * distances[-1] - 1 < size // 2 - 1:
        distances.append(2 * distances[-1])
    last = distances[-1]
    gains = size & (size - 1) == 0 and len(distances) > 1

    def spread(outer, msg, forward):
        carry = gains and not forward
        if last == 2:
            pair = exchange(msg, blocks(size, 1, 0))
            far = exchange(msg, [(i, i + 3) for i in range(1, size - 3, 2)])
            (msg,) = call(
                functools.partial(pair_body, forward, carry), [(message, BF16)], "vvvv", flops=0, moved=1 << 20
            )(number, outer, msg, pair)
            return [pair, far, *swaps(msg, last)], msg
        terms = []
        for distance in distances[:-1]:
            even, odd = swaps(msg, distance)
            *terms, msg = call(
                functools.partial(merge_body, distance, forward, carry), [(summed, F32), (message, BF16)],
                "vvvvv" + "v" * len(terms), flops=0, moved=1 << 20,
            )(number, outer, msg, *terms, even, odd)
        return [*terms, *swaps(msg, last)], msg

    in_hbm = lambda block: pltpu.with_memory_space_constraint(block, pltpu.HBM)
    query, key, value, w, number, outer, msg = call(
        functools.partial(opening_body, heads, dim),
        [(rows, BF16)] * 3 + [((width, model), BF16), ((8, dim), F32), (summed, F32), (message, BF16)],
        "vhhhh", flops=matrix, moved=4 << 20, scratch=[pltpu.SemaphoreType.DMA((4,))],
    )(stretch_doc, *map(in_hbm, (queries[0], key_rows[0], value_rows[0], w_out)))
    weights, within, normed_grad = call(
        functools.partial(local_body, heads, dim),
        [((heads * tokens, tokens), BF16), (rows, F32), (rows, F32)],
        "vvvhv", flops=2 * square + 2 * layer, moved=6 << 20,
        scratch=[pltpu.VMEM((tokens, model), BF16), pltpu.SemaphoreType.DMA],
    )(query, key, value, in_hbm(cotangent[0]), w)
    sums, _ = spread(outer, msg, True)
    state, keep, send, grad, outer, msg, gain_part = call(
        functools.partial(forward_body, heads, dim, last),
        [
            (summed, BF16), ((tokens // 2, width), BF16), (half, BF16),
            (rows, BF16), (summed, F32), (message, BF16), (small, F32),
        ],
        "vvvvvv" + "v" * len(sums), flops=2 * matrix + layer, moved=4 << 20, scratch=[pltpu.VMEM(rows, BF16)],
    )(number, query, within, normed_grad, head_gain, w, *sums)
    got = lax.ppermute(send, "head", [(0, 1), (1, 0)])
    query_grad, key_part, value_part = call(
        functools.partial(backward_body, heads, dim),
        [(rows, BF16), (rows, F32), (rows, F32)],
        "vvvvvv", flops=4 * square + matrix, moved=4 << 20,
    )(query, key, value, weights, grad, state)
    sums, msg = spread(outer, msg, False)
    if gains:
        (gain,) = call(gain_body, [(small, F32)], "vv", flops=0, moved=1 << 16)(msg, sums[-2])
        across = [flipped(gain, *to) for to in ((0, 1), (size // 2, 0), (size // 2, 1))]
        gain_parts = [gain, *across]
    else:
        gain_parts = [lax.psum(gain_part, ("seq", "dp"))]
    key_grad, value_grad = call(
        functools.partial(last_body, heads, dim, last), [(rows, BF16), (rows, BF16)],
        "vvvvv" + "v" * len(sums), flops=2 * matrix, moved=3 << 20,
    )(number, key, value, key_part, value_part, *sums)
    scale = 1.0 / math.sqrt(size * lax.axis_size("dp") * tokens)
    layer_out, gain_grad = call(
        functools.partial(layer_body, scale), [(half, BF16), (small, F32)],
        "vvv" + "v" * len(gain_parts), flops=layer, moved=6 << 20,
    )(keep, w, got, *gain_parts)
    return layer_out[None], query_grad[None], key_grad[None], value_grad[None], gain_grad


def solution(mesh):
    rows = P("dp", "seq", "head")
    return jax.shard_map(
        on_device,
        mesh=mesh,
        in_specs=(rows, rows, rows, P("dp", "seq"), P("head", None), P("head", None), P("dp", "seq", None)),
        out_specs=(P("dp", ("seq", "head"), None), rows, rows, rows, P("head", None)),
        check_vma=False,
    )
```

```python
import functools
import math

import jax
import jax.numpy as jnp
from jax import lax
from jax.experimental import pallas as pl
from jax.experimental.pallas import tpu as pltpu
from jax.sharding import PartitionSpec as P

EPSILON = 1e-05
F32 = jnp.float32
BF16 = jnp.bfloat16
TAIL = 16
GAIN = 4


def nn(a, b):
    return lax.dot_general(a, b, (((1,), (0,)), ((), ())), preferred_element_type=F32)


def nt(a, b):
    return lax.dot_general(a, b, (((1,), (1,)), ((), ())), preferred_element_type=F32)


def tn(a, b):
    return lax.dot_general(a, b, (((0,), (0,)), ((), ())), preferred_element_type=F32)


def call(body, outs, places, flops, moved, scratch=()):
    space = {"a": pl.ANY, "v": pltpu.VMEM, "h": pltpu.HBM}
    return pl.pallas_call(
        body,
        out_shape=[jax.ShapeDtypeStruct(s, t) for s, t in outs],
        in_specs=[pl.BlockSpec(memory_space=space[p]) for p in places],
        out_specs=[pl.BlockSpec(memory_space=pltpu.VMEM) for _ in outs],
        scratch_shapes=list(scratch),
        cost_estimate=pl.CostEstimate(flops=flops, bytes_accessed=moved, transcendentals=0),
        compiler_params=pltpu.CompilerParams(vmem_limit_bytes=40 << 20),
    )


def pairing(size, pairs):
    partner = {i: (j, False) for a, b in pairs for i, j in ((a, b), (b, a))}
    route = []
    for i in range(size):
        to, same_stretch = partner.get(i, (i, True))
        route += [(2 * i + core, 2 * to + (core ^ same_stretch)) for core in (0, 1)]
    return route


def exchange(block, pairs):
    return lax.ppermute(block, ("seq", "dp"), pairing(lax.axis_size("seq"), pairs))


def blocks(size, distance, odd):
    return [(i, i + distance) for i in range(size - distance) if (i // distance) % 2 == odd]


def swaps(block, distance):
    size = lax.axis_size("seq")
    return [exchange(block, blocks(size, distance, odd)) for odd in (0, 1)]


def flipped(block, distance, cores):
    route = [
        (2 * i + core, 2 * (i ^ distance) + (core ^ cores))
        for i in range(lax.axis_size("seq"))
        for core in (0, 1)
    ]
    return lax.ppermute(block, ("seq", "dp"), route)


def put_tail(msg_ref, number, gain=None):
    rows, dim = msg_ref.shape[0] - TAIL, msg_ref.shape[1]
    high = jnp.zeros((GAIN, dim), F32) if gain is None else gain.astype(BF16).astype(F32)
    low = jnp.zeros((GAIN, dim), F32) if gain is None else gain - high
    low = low.astype(BF16).astype(F32)
    number = jnp.broadcast_to(number, (TAIL - 2 * GAIN, dim))
    msg_ref[rows:, :] = jnp.concatenate([high, low, number], axis=0).astype(BF16)
    return high + low


def sent_gain(msg_ref):
    tail = msg_ref[msg_ref.shape[0] - TAIL :, :].astype(F32)
    return tail[:GAIN, :] + tail[GAIN : 2 * GAIN, :]


def opened(msg):
    msg = msg.astype(F32)
    rows = msg.shape[0] - TAIL
    return msg[:rows, :], msg[rows + 2 * GAIN : rows + 2 * GAIN + 1, :]


def taken(even_ref, odd_ref, number, distance, forward):
    me, size = lax.axis_index("seq"), lax.axis_size("seq")
    upper = lax.rem(lax.div(me, distance), 2)
    from_odd = upper == 0 if forward else upper == 1
    there = me >= distance if forward else me + distance < size
    sums, theirs = opened(jnp.where(from_odd, odd_ref[...], even_ref[...]))
    return jnp.where(theirs == jnp.where(there, number, -1.0), sums, 0.0)


def beside(pair_ref, far_ref, number, forward):
    me, size = lax.axis_index("seq"), lax.axis_size("seq")
    in_pair = lax.rem(me, 2) == (1 if forward else 0)
    there = in_pair | (me >= 3 if forward else me + 3 < size)
    sums, theirs = opened(jnp.where(in_pair, pair_ref[...], far_ref[...]))
    return jnp.where(theirs == jnp.where(there, number, -1.0), sums, 0.0)


def total(refs, number, distance, forward):
    *near, even_ref, odd_ref = refs
    if len(near) == 1:
        first = near[0][...]
    else:
        first = beside(*near, number, forward)
    return first + taken(even_ref, odd_ref, number, distance, forward)


def opening_body(
    heads, dim, doc_any, key_hbm, value_hbm,
    key_ref, value_ref, number_ref, sum_ref, msg_ref, doc_ref, sems,
):
    copies = [
        pltpu.make_async_copy(src, dst, sems.at[i])
        for i, (src, dst) in enumerate(((key_hbm, key_ref), (value_hbm, value_ref), (doc_any, doc_ref)))
    ]
    for copy in copies:
        copy.start()
    copies[2].wait()
    number = jnp.full(number_ref.shape, doc_ref[0, 0] + 1, jnp.int32).astype(F32)
    number_ref[...] = number
    put_tail(msg_ref, number[:1, :])
    copies[0].wait()
    copies[1].wait()
    for h in range(heads):
        cols, rows = slice(h * dim, (h + 1) * dim), slice(h * dim, (h + 1) * dim)
        sums = tn(key_ref[:, cols], value_ref[:, cols])
        sum_ref[rows, :] = sums
        msg_ref[rows, :] = sums.astype(BF16)


def local_body(
    heads, dim, query_hbm, key_ref, value_ref, cot_hbm, w_hbm,
    query_ref, w_ref, weight_ref, within_ref, normed_grad_ref, cot_ref, sems,
):
    copies = [
        pltpu.make_async_copy(src, dst, sems.at[i])
        for i, (src, dst) in enumerate(((query_hbm, query_ref), (cot_hbm, cot_ref), (w_hbm, w_ref)))
    ]
    for copy in copies:
        copy.start()
    tokens = query_ref.shape[0]
    causal = lax.broadcasted_iota(jnp.int32, (tokens, tokens), 0) >= lax.broadcasted_iota(
        jnp.int32, (tokens, tokens), 1
    )
    copies[0].wait()
    for h in range(heads):
        cols = slice(h * dim, (h + 1) * dim)
        scores = nt(query_ref[:, cols], key_ref[:, cols])
        weights = jnp.where(causal, scores, 0.0).astype(BF16)
        weight_ref[h * tokens : (h + 1) * tokens, :] = weights
        within_ref[:, cols] = nn(weights, value_ref[:, cols])
    copies[1].wait()
    copies[2].wait()
    normed_grad_ref[...] = nt(cot_ref[...], w_ref[...])


def merge_gain(gains, own_ref, other_ref):
    return sent_gain(own_ref) + sent_gain(other_ref) if gains else None


def pair_body(forward, gains, number_ref, sum_ref, own_ref, pair_ref, msg_ref):
    rows = sum_ref.shape[0]
    number = number_ref[:1, :]
    leads = lax.rem(lax.axis_index("seq"), 2) == (1 if forward else 0)
    sums, theirs = opened(pair_ref[...])
    mine = sum_ref[...]
    same = theirs == number
    keep_mine, keep_theirs = same | leads, same | jnp.logical_not(leads)
    msg_ref[:rows, :] = (jnp.where(keep_mine, mine, 0.0) + jnp.where(keep_theirs, sums, 0.0)).astype(BF16)
    put_tail(msg_ref, jnp.where(leads, number, theirs), merge_gain(gains, own_ref, pair_ref))


def merge_body(distance, forward, gains, number_ref, sum_ref, own_ref, *refs):
    *term_ref, even_ref, odd_ref, out_ref, msg_ref = refs
    rows = sum_ref.shape[0]
    number = number_ref[:1, :]
    term = taken(even_ref, odd_ref, number, distance, forward)
    if term_ref:
        term = term + term_ref[0][...]
    out_ref[...] = term
    msg_ref[:rows, :] = (sum_ref[...] + term).astype(BF16)
    put_tail(msg_ref, number, merge_gain(gains, own_ref, even_ref))


def gain_body(own_ref, other_ref, out_ref):
    out_ref[...] = merge_gain(True, own_ref, other_ref)


def forward_body(
    heads, dim, distance, number_ref, query_ref, within_ref, normed_grad_ref, gain_ref, w_ref, *refs
):
    *sum_refs, state_ref, keep_ref, send_ref, grad_ref, outer_ref, msg_ref, gain_grad_ref, normed_ref = refs
    half = keep_ref.shape[0]
    number = number_ref[:1, :]
    state_ref[...] = total(sum_refs, number, distance, True).astype(BF16)
    for h in range(heads):
        cols, rows = slice(h * dim, (h + 1) * dim), slice(h * dim, (h + 1) * dim)
        query = query_ref[:, cols]
        attended = within_ref[:, cols] + nn(query, state_ref[rows, :])
        inv_rms = lax.rsqrt(jnp.mean(attended * attended, axis=-1, keepdims=True) + EPSILON)
        unit = attended * inv_rms
        gain = gain_ref[h : h + 1, :]
        normed_ref[:, cols] = (unit * gain).astype(BF16)
        normed_grad = normed_grad_ref[:, cols]
        gain_grad_ref[h : h + 1, :] = jnp.sum(normed_grad * unit, axis=0, keepdims=True)
        scaled = normed_grad * gain
        grad = inv_rms * (scaled - unit * jnp.mean(scaled * unit, axis=-1, keepdims=True))
        grad = grad.astype(BF16)
        grad_ref[:, cols] = grad
        outer = tn(query, grad)
        outer_ref[rows, :] = outer
        msg_ref[rows, :] = outer.astype(BF16)
    put_tail(msg_ref, number, gain_grad_ref[...])
    head = lax.axis_index("head")
    keep_ref[...] = normed_ref[pl.ds(pl.multiple_of(head * half, half), half), :]
    send_ref[...] = nn(
        normed_ref[pl.ds(pl.multiple_of((1 - head) * half, half), half), :], w_ref[...]
    ).astype(BF16)


def backward_body(
    heads, dim, query_ref, key_ref, value_ref, weight_ref, grad_ref, state_ref,
    query_grad_ref, key_part_ref, value_part_ref,
):
    tokens = query_ref.shape[0]
    causal = lax.broadcasted_iota(jnp.int32, (tokens, tokens), 0) >= lax.broadcasted_iota(
        jnp.int32, (tokens, tokens), 1
    )
    for h in range(heads):
        cols, rows = slice(h * dim, (h + 1) * dim), slice(h * dim, (h + 1) * dim)
        grad = grad_ref[:, cols]
        grad_scores = nt(grad, value_ref[:, cols])
        grad_weights = jnp.where(causal, grad_scores, 0.0).astype(BF16)
        query_grad_ref[:, cols] = (
            nn(grad_weights, key_ref[:, cols]) + nt(grad, state_ref[rows, :])
        ).astype(BF16)
        key_part_ref[:, cols] = tn(grad_weights, query_ref[:, cols])
        value_part_ref[:, cols] = tn(weight_ref[h * tokens : (h + 1) * tokens, :], grad)


def last_body(
    heads, dim, distance, number_ref, key_ref, value_ref, key_part_ref, value_part_ref, *refs
):
    *sum_refs, key_grad_ref, value_grad_ref = refs
    state = total(sum_refs, number_ref[:1, :], distance, False).astype(BF16)
    for h in range(heads):
        cols, rows = slice(h * dim, (h + 1) * dim), slice(h * dim, (h + 1) * dim)
        key_grad_ref[:, cols] = (
            key_part_ref[:, cols] + nt(value_ref[:, cols], state[rows, :])
        ).astype(BF16)
        value_grad_ref[:, cols] = (
            value_part_ref[:, cols] + nn(key_ref[:, cols], state[rows, :])
        ).astype(BF16)


def layer_body(scale, keep_ref, w_ref, got_ref, *refs):
    *gain_refs, out_ref, gain_grad_ref = refs
    out_ref[...] = (nn(keep_ref[...], w_ref[...]) + got_ref[...].astype(F32)).astype(BF16)
    parts = [ref[...] for ref in gain_refs]
    if len(parts) == 4:
        parts = [(parts[0] + parts[1]) + (parts[2] + parts[3])]
    gain_grad_ref[...] = parts[0] * scale


def on_device(queries, key_rows, value_rows, stretch_doc, head_gain, w_out, cotangent):
    tokens, width = queries.shape[1:]
    heads, dim = head_gain.shape
    model = w_out.shape[1]
    size = lax.axis_size("seq")
    matrix = 2 * tokens * dim * dim * heads
    square = 2 * tokens * tokens * dim * heads
    layer = tokens * width * model
    rows, summed, message = (tokens, width), (heads * dim, dim), (heads * dim + TAIL, dim)
    small, half = (heads, dim), (tokens // 2, model)
    distances = [1]
    while 2 * distances[-1] - 1 < size // 2 - 1:
        distances.append(2 * distances[-1])
    last = distances[-1]
    gains = size & (size - 1) == 0 and len(distances) > 1

    def spread(outer, msg, forward):
        carry = gains and not forward
        if last == 2:
            pair = exchange(msg, blocks(size, 1, 0))
            far = exchange(msg, [(i, i + 3) for i in range(1, size - 3, 2)])
            (msg,) = call(
                functools.partial(pair_body, forward, carry), [(message, BF16)], "vvvv", flops=0, moved=1 << 20
            )(number, outer, msg, pair)
            even, odd = swaps(msg, last)
            even, far = lax.optimization_barrier((even, far))
            return [pair, far, even, odd], msg
        terms = []
        for distance in distances[:-1]:
            even, odd = swaps(msg, distance)
            *terms, msg = call(
                functools.partial(merge_body, distance, forward, carry), [(summed, F32), (message, BF16)],
                "vvvvv" + "v" * len(terms), flops=0, moved=1 << 20,
            )(number, outer, msg, *terms, even, odd)
        return [*terms, *swaps(msg, last)], msg

    in_hbm = lambda block: pltpu.with_memory_space_constraint(block, pltpu.HBM)
    key, value, number, outer, msg = call(
        functools.partial(opening_body, heads, dim),
        [(rows, BF16)] * 2 + [((8, dim), F32), (summed, F32), (message, BF16)],
        "ahh", flops=matrix, moved=1 << 20, scratch=[pltpu.SMEM((1, 1), jnp.int32), pltpu.SemaphoreType.DMA((3,))],
    )(stretch_doc, in_hbm(key_rows[0]), in_hbm(value_rows[0]))
    query, w, weights, within, normed_grad = call(
        functools.partial(local_body, heads, dim),
        [(rows, BF16), ((width, model), BF16), ((heads * tokens, tokens), BF16), (rows, F32), (rows, F32)],
        "hvvhh", flops=2 * square + 2 * layer, moved=6 << 20,
        scratch=[pltpu.VMEM((tokens, model), BF16), pltpu.SemaphoreType.DMA((3,))],
    )(in_hbm(queries[0]), key, value, in_hbm(cotangent[0]), in_hbm(w_out))
    sums, _ = spread(outer, msg, True)
    state, keep, send, grad, outer, msg, gain_part = call(
        functools.partial(forward_body, heads, dim, last),
        [
            (summed, BF16), ((tokens // 2, width), BF16), (half, BF16),
            (rows, BF16), (summed, F32), (message, BF16), (small, F32),
        ],
        "vvvvvv" + "v" * len(sums), flops=2 * matrix + layer, moved=4 << 20, scratch=[pltpu.VMEM(rows, BF16)],
    )(number, query, within, normed_grad, head_gain, w, *sums)
    got = lax.ppermute(send, "head", [(0, 1), (1, 0)])
    query_grad, key_part, value_part = call(
        functools.partial(backward_body, heads, dim),
        [(rows, BF16), (rows, F32), (rows, F32)],
        "vvvvvv", flops=0, moved=1 << 16,
    )(query, key, value, weights, grad, state)
    sums, msg = spread(outer, msg, False)
    if gains:
        (gain,) = call(gain_body, [(small, F32)], "vv", flops=0, moved=1 << 16)(msg, sums[-2])
        across = [flipped(gain, *to) for to in ((0, 1), (size // 2, 0), (size // 2, 1))]
        gain_parts = [gain, *across]
    else:
        gain_parts = [lax.psum(gain_part, ("seq", "dp"))]
    key_grad, value_grad = call(
        functools.partial(last_body, heads, dim, last), [(rows, BF16), (rows, BF16)],
        "vvvvv" + "v" * len(sums), flops=2 * matrix, moved=3 << 20,
    )(number, key, value, key_part, value_part, *sums)
    scale = 1.0 / math.sqrt(size * lax.axis_size("dp") * tokens)
    layer_out, gain_grad = call(
        functools.partial(layer_body, scale), [(half, BF16), (small, F32)],
        "vvv" + "v" * len(gain_parts), flops=layer, moved=6 << 20,
    )(keep, w, got, *gain_parts)
    return layer_out[None], query_grad[None], key_grad[None], value_grad[None], gain_grad


def solution(mesh):
    rows = P("dp", "seq", "head")
    return jax.shard_map(
        on_device,
        mesh=mesh,
        in_specs=(rows, rows, rows, P("dp", "seq"), P("head", None), P("head", None), P("dp", "seq", None)),
        out_specs=(P("dp", ("seq", "head"), None), rows, rows, rows, P("head", None)),
        check_vma=False,
    )
```

```python
import functools
import math

import jax
import jax.numpy as jnp
from jax import lax
from jax.experimental import pallas as pl
from jax.experimental.pallas import tpu as pltpu
from jax.sharding import PartitionSpec as P

EPSILON = 1e-05
F32 = jnp.float32
BF16 = jnp.bfloat16
TAIL = 16
GAIN = 4


def nn(a, b):
    return lax.dot_general(a, b, (((1,), (0,)), ((), ())), preferred_element_type=F32)


def nt(a, b):
    return lax.dot_general(a, b, (((1,), (1,)), ((), ())), preferred_element_type=F32)


def tn(a, b):
    return lax.dot_general(a, b, (((0,), (0,)), ((), ())), preferred_element_type=F32)


def call(body, outs, places, flops, moved, scratch=()):
    space = {"a": pl.ANY, "v": pltpu.VMEM, "h": pltpu.HBM}
    return pl.pallas_call(
        body,
        out_shape=[jax.ShapeDtypeStruct(s, t) for s, t in outs],
        in_specs=[pl.BlockSpec(memory_space=space[p]) for p in places],
        out_specs=[pl.BlockSpec(memory_space=pltpu.VMEM) for _ in outs],
        scratch_shapes=list(scratch),
        name=getattr(body, "func", body).__name__,
        cost_estimate=pl.CostEstimate(flops=flops, bytes_accessed=moved, transcendentals=0),
        compiler_params=pltpu.CompilerParams(vmem_limit_bytes=40 << 20),
    )


def pairing(size, pairs):
    partner = {i: (j, False) for a, b in pairs for i, j in ((a, b), (b, a))}
    route = []
    for i in range(size):
        to, same_stretch = partner.get(i, (i, True))
        route += [(2 * i + core, 2 * to + (core ^ same_stretch)) for core in (0, 1)]
    return route


def exchange(block, pairs):
    return lax.ppermute(block, ("seq", "dp"), pairing(lax.axis_size("seq"), pairs))


def blocks(size, distance, odd):
    return [(i, i + distance) for i in range(size - distance) if (i // distance) % 2 == odd]


def swaps(block, distance):
    size = lax.axis_size("seq")
    return [exchange(block, blocks(size, distance, odd)) for odd in (0, 1)]


def flipped(block, distance, cores):
    route = [
        (2 * i + core, 2 * (i ^ distance) + (core ^ cores))
        for i in range(lax.axis_size("seq"))
        for core in (0, 1)
    ]
    return lax.ppermute(block, ("seq", "dp"), route)


def put_tail(msg_ref, number, gain=None):
    rows, dim = msg_ref.shape[0] - TAIL, msg_ref.shape[1]
    high = jnp.zeros((GAIN, dim), F32) if gain is None else gain.astype(BF16).astype(F32)
    low = jnp.zeros((GAIN, dim), F32) if gain is None else gain - high
    low = low.astype(BF16).astype(F32)
    number = jnp.broadcast_to(number, (TAIL - 2 * GAIN, dim))
    msg_ref[rows:, :] = jnp.concatenate([high, low, number], axis=0).astype(BF16)
    return high + low


def sent_gain(msg_ref):
    tail = msg_ref[msg_ref.shape[0] - TAIL :, :].astype(F32)
    return tail[:GAIN, :] + tail[GAIN : 2 * GAIN, :]


def opened(msg):
    msg = msg.astype(F32)
    rows = msg.shape[0] - TAIL
    return msg[:rows, :], msg[rows + 2 * GAIN : rows + 2 * GAIN + 1, :]


def taken(even_ref, odd_ref, number, distance, forward):
    me, size = lax.axis_index("seq"), lax.axis_size("seq")
    upper = lax.rem(lax.div(me, distance), 2)
    from_odd = upper == 0 if forward else upper == 1
    there = me >= distance if forward else me + distance < size
    sums, theirs = opened(jnp.where(from_odd, odd_ref[...], even_ref[...]))
    return jnp.where(theirs == jnp.where(there, number, -1.0), sums, 0.0)


def beside(pair_ref, far_ref, number, forward):
    me, size = lax.axis_index("seq"), lax.axis_size("seq")
    in_pair = lax.rem(me, 2) == (1 if forward else 0)
    there = in_pair | (me >= 3 if forward else me + 3 < size)
    sums, theirs = opened(jnp.where(in_pair, pair_ref[...], far_ref[...]))
    return jnp.where(theirs == jnp.where(there, number, -1.0), sums, 0.0)


def total(refs, number, distance, forward):
    *near, even_ref, odd_ref = refs
    if len(near) == 1:
        first = near[0][...]
    else:
        first = beside(*near, number, forward)
    return first + taken(even_ref, odd_ref, number, distance, forward)


def opening_body(
    heads, dim, doc_any, key_hbm, value_hbm,
    key_ref, value_ref, number_ref, sum_ref, msg_ref, doc_ref, sems,
):
    copies = [
        pltpu.make_async_copy(src, dst, sems.at[i])
        for i, (src, dst) in enumerate(((key_hbm, key_ref), (value_hbm, value_ref), (doc_any, doc_ref)))
    ]
    for copy in copies:
        copy.start()
    copies[2].wait()
    number = jnp.full(number_ref.shape, doc_ref[0, 0] + 1, jnp.int32).astype(F32)
    number_ref[...] = number
    put_tail(msg_ref, number[:1, :])
    copies[0].wait()
    copies[1].wait()
    for h in range(heads):
        cols, rows = slice(h * dim, (h + 1) * dim), slice(h * dim, (h + 1) * dim)
        sums = tn(key_ref[:, cols], value_ref[:, cols])
        sum_ref[rows, :] = sums
        msg_ref[rows, :] = sums.astype(BF16)


def local_body(
    heads, dim, query_hbm, key_ref, value_ref, cot_hbm, w_hbm,
    query_ref, w_ref, weight_ref, within_ref, normed_grad_ref, cot_ref, sems,
):
    copies = [
        pltpu.make_async_copy(src, dst, sems.at[i])
        for i, (src, dst) in enumerate(((query_hbm, query_ref), (cot_hbm, cot_ref), (w_hbm, w_ref)))
    ]
    for copy in copies:
        copy.start()
    tokens = query_ref.shape[0]
    causal = lax.broadcasted_iota(jnp.int32, (tokens, tokens), 0) >= lax.broadcasted_iota(
        jnp.int32, (tokens, tokens), 1
    )
    copies[0].wait()
    for h in range(heads):
        cols = slice(h * dim, (h + 1) * dim)
        scores = nt(query_ref[:, cols], key_ref[:, cols])
        weights = jnp.where(causal, scores, 0.0).astype(BF16)
        weight_ref[h * tokens : (h + 1) * tokens, :] = weights
        within_ref[:, cols] = nn(weights, value_ref[:, cols])
    copies[1].wait()
    copies[2].wait()
    normed_grad_ref[...] = nt(cot_ref[...], w_ref[...])


def fetch_body(number_ref, w_hbm, part_ref, sem):
    rows, cols = part_ref.shape
    core = lax.axis_index("dp")
    ours = w_hbm.at[pl.ds(pl.multiple_of(core * rows, rows), rows), pl.ds(0, cols)]
    copy = pltpu.make_async_copy(ours, part_ref, sem)
    copy.start()
    copy.wait()


def merge_gain(gains, own_ref, other_ref):
    return sent_gain(own_ref) + sent_gain(other_ref) if gains else None


def pair_body(forward, gains, number_ref, sum_ref, own_ref, pair_ref, msg_ref, *gain_ref):
    rows = sum_ref.shape[0]
    number = number_ref[:1, :]
    leads = lax.rem(lax.axis_index("seq"), 2) == (1 if forward else 0)
    sums, theirs = opened(pair_ref[...])
    mine = sum_ref[...]
    same = theirs == number
    keep_mine, keep_theirs = same | leads, same | jnp.logical_not(leads)
    msg_ref[:rows, :] = (jnp.where(keep_mine, mine, 0.0) + jnp.where(keep_theirs, sums, 0.0)).astype(BF16)
    gain = put_tail(msg_ref, jnp.where(leads, number, theirs), merge_gain(gains, own_ref, pair_ref))
    if gains:
        gain_ref[0][...] = gain


def merge_body(distance, forward, gains, number_ref, sum_ref, own_ref, *refs):
    gain_ref, refs = (refs[-1:], refs[:-1]) if gains else ((), refs)
    *term_ref, even_ref, odd_ref, out_ref, msg_ref = refs
    rows = sum_ref.shape[0]
    number = number_ref[:1, :]
    term = taken(even_ref, odd_ref, number, distance, forward)
    if term_ref:
        term = term + term_ref[0][...]
    out_ref[...] = term
    msg_ref[:rows, :] = (sum_ref[...] + term).astype(BF16)
    gain = put_tail(msg_ref, number, merge_gain(gains, own_ref, even_ref))
    if gains:
        gain_ref[0][...] = gain


def gain_body(own_ref, other_ref, far_ref, farther_ref, out_ref):
    out_ref[...] = merge_gain(True, own_ref, other_ref) + (far_ref[...] + farther_ref[...])


def forward_body(
    heads, dim, distance, number_ref, query_ref, within_ref, normed_grad_ref, gain_ref, w_ref, *refs
):
    *sum_refs, state_ref, keep_ref, give_ref, grad_ref, outer_ref, msg_ref, gain_grad_ref, normed_ref = refs
    half, width = keep_ref.shape
    number = number_ref[:1, :]
    state_ref[...] = total(sum_refs, number, distance, True).astype(BF16)
    for h in range(heads):
        cols, rows = slice(h * dim, (h + 1) * dim), slice(h * dim, (h + 1) * dim)
        query = query_ref[:, cols]
        attended = within_ref[:, cols] + nn(query, state_ref[rows, :])
        inv_rms = lax.rsqrt(jnp.mean(attended * attended, axis=-1, keepdims=True) + EPSILON)
        unit = attended * inv_rms
        gain = gain_ref[h : h + 1, :]
        normed_ref[:, cols] = (unit * gain).astype(BF16)
        normed_grad = normed_grad_ref[:, cols]
        gain_grad_ref[h : h + 1, :] = jnp.sum(normed_grad * unit, axis=0, keepdims=True)
        scaled = normed_grad * gain
        grad = inv_rms * (scaled - unit * jnp.mean(scaled * unit, axis=-1, keepdims=True))
        grad = grad.astype(BF16)
        grad_ref[:, cols] = grad
        outer = tn(query, grad)
        outer_ref[rows, :] = outer
        msg_ref[rows, :] = outer.astype(BF16)
    put_tail(msg_ref, number, gain_grad_ref[...])
    head = lax.axis_index("head")
    keep_ref[...] = normed_ref[pl.ds(pl.multiple_of(head * half, half), half), :]
    give = normed_ref[pl.ds(pl.multiple_of((1 - head) * half, half), half), :]
    give_ref[:, :width] = give
    give_ref[:, width:] = nn(give, w_ref[:, w_ref.shape[1] + width - give_ref.shape[1] :]).astype(BF16)


def backward_body(
    heads, dim, query_ref, key_ref, value_ref, weight_ref, grad_ref, state_ref,
    query_grad_ref, key_part_ref, value_part_ref,
):
    tokens = query_ref.shape[0]
    causal = lax.broadcasted_iota(jnp.int32, (tokens, tokens), 0) >= lax.broadcasted_iota(
        jnp.int32, (tokens, tokens), 1
    )
    for h in range(heads):
        cols, rows = slice(h * dim, (h + 1) * dim), slice(h * dim, (h + 1) * dim)
        grad = grad_ref[:, cols]
        grad_scores = nt(grad, value_ref[:, cols])
        grad_weights = jnp.where(causal, grad_scores, 0.0).astype(BF16)
        query_grad_ref[:, cols] = (
            nn(grad_weights, key_ref[:, cols]) + nt(grad, state_ref[rows, :])
        ).astype(BF16)
        key_part_ref[:, cols] = tn(grad_weights, query_ref[:, cols])
        value_part_ref[:, cols] = tn(weight_ref[h * tokens : (h + 1) * tokens, :], grad)


def last_body(
    heads, dim, distance, number_ref, key_ref, value_ref, key_part_ref, value_part_ref, *refs
):
    *sum_refs, key_grad_ref, value_grad_ref = refs
    state = total(sum_refs, number_ref[:1, :], distance, False).astype(BF16)
    for h in range(heads):
        cols, rows = slice(h * dim, (h + 1) * dim), slice(h * dim, (h + 1) * dim)
        key_grad_ref[:, cols] = (
            key_part_ref[:, cols] + nt(value_ref[:, cols], state[rows, :])
        ).astype(BF16)
        value_grad_ref[:, cols] = (
            value_part_ref[:, cols] + nn(key_ref[:, cols], state[rows, :])
        ).astype(BF16)


def layer_body(scale, keep_ref, w_ref, took_ref, mine_ref, other_ref, *refs):
    *gain_refs, out_ref, gain_grad_ref = refs
    width, cols = mine_ref.shape
    core = lax.axis_index("dp")
    at = lambda i: pl.ds(pl.multiple_of(i * width, width), width)
    keep = keep_ref[...]
    out_ref[:, :cols] = (
        nn(keep, w_ref[:, :cols])
        + nn(took_ref[:, at(core)], mine_ref[...])
        + nn(took_ref[:, at(1 - core)], other_ref[...])
    ).astype(BF16)
    out_ref[:, cols:] = (nn(keep, w_ref[:, cols:]) + took_ref[:, 2 * width :].astype(F32)).astype(BF16)
    gain = gain_refs[0][...]
    if len(gain_refs) > 1:
        gain = gain + gain_refs[1][...]
    gain_grad_ref[...] = gain * scale


def on_device(queries, key_rows, value_rows, stretch_doc, head_gain, w_out, cotangent):
    tokens, width = queries.shape[1:]
    heads, dim = head_gain.shape
    model = w_out.shape[1]
    size = lax.axis_size("seq")
    matrix = 2 * tokens * dim * dim * heads
    square = 2 * tokens * tokens * dim * heads
    layer = tokens * width * model
    rows, summed, message = (tokens, width), (heads * dim, dim), (heads * dim + TAIL, dim)
    small, half, cols = (heads, dim), tokens // 2, model // 2
    distances = [1]
    while 2 * distances[-1] - 1 < size // 2 - 1:
        distances.append(2 * distances[-1])
    last = distances[-1]
    gains = size & (size - 1) == 0 and len(distances) > 1

    def spread(outer, msg, forward):
        carry = gains and not forward
        extra = [(small, F32)] * carry
        if last == 2:
            pair = exchange(msg, blocks(size, 1, 0))
            far = exchange(msg, [(i, i + 3) for i in range(1, size - 3, 2)])
            msg, *gain = call(
                functools.partial(pair_body, forward, carry), [(message, BF16), *extra], "vvvv", flops=0, moved=1 << 20
            )(number, outer, msg, pair)
            even, odd = swaps(msg, last)
            even, odd, far = lax.optimization_barrier((even, odd, far))
            return [pair, far, even, odd], msg, gain
        terms = []
        for distance in distances[:-1]:
            even, odd = swaps(msg, distance)
            term, msg, *gain = call(
                functools.partial(merge_body, distance, forward, carry), [(summed, F32), (message, BF16), *extra],
                "vvvvv" + "v" * len(terms), flops=0, moved=1 << 20,
            )(number, outer, msg, *terms, even, odd)
            terms = [term]
        return [*terms, *swaps(msg, last)], msg, gain

    in_hbm = lambda block: pltpu.with_memory_space_constraint(block, pltpu.HBM)
    key, value, number, outer, msg = call(
        functools.partial(opening_body, heads, dim),
        [(rows, BF16)] * 2 + [((8, dim), F32), (summed, F32), (message, BF16)],
        "ahh", flops=matrix, moved=1 << 20, scratch=[pltpu.SMEM((1, 1), jnp.int32), pltpu.SemaphoreType.DMA((3,))],
    )(stretch_doc, in_hbm(key_rows[0]), in_hbm(value_rows[0]))
    (part,) = call(fetch_body, [((width // 2, cols), BF16)], "vh", flops=0, moved=1 << 20, scratch=[pltpu.SemaphoreType.DMA])(
        number, in_hbm(w_out)
    )
    across = [(0, 1), (1, 0)]
    mine = lax.ppermute(part, "head", across)
    query, w, weights, within, normed_grad = call(
        functools.partial(local_body, heads, dim),
        [(rows, BF16), ((width, model), BF16), ((heads * tokens, tokens), BF16), (rows, F32), (rows, F32)],
        "hvvhh", flops=2 * square + 2 * layer, moved=6 << 20,
        scratch=[pltpu.VMEM((tokens, model), BF16), pltpu.SemaphoreType.DMA((3,))],
    )(in_hbm(queries[0]), key, value, in_hbm(cotangent[0]), in_hbm(w_out))
    sums, _, _ = spread(outer, msg, True)
    state, keep, give, grad, outer, msg, gain_part = call(
        functools.partial(forward_body, heads, dim, last),
        [
            (summed, BF16), ((half, width), BF16), ((half, width + model - cols), BF16),
            (rows, BF16), (summed, F32), (message, BF16), (small, F32),
        ],
        "vvvvvv" + "v" * len(sums), flops=2 * matrix + layer, moved=4 << 20, scratch=[pltpu.VMEM(rows, BF16)],
    )(number, query, within, normed_grad, head_gain, w, *sums)
    took = lax.ppermute(give, "head", across)
    query_grad, key_part, value_part = call(
        functools.partial(backward_body, heads, dim),
        [(rows, BF16), (rows, F32), (rows, F32)],
        "vvvvvv", flops=0, moved=1 << 16,
    )(query, key, value, weights, grad, state)
    sums, msg, gain = spread(outer, msg, False)
    if gains:
        *sums, key_part, took = lax.optimization_barrier((*sums, key_part, took))
        far = [flipped(gain[0], to, 0) for to in (size // 2, size // 2 + last)]
        (gain,) = call(gain_body, [(small, F32)], "vvvv", flops=0, moved=1 << 16)(msg, sums[-2], *far)
        gain, mine = lax.optimization_barrier((gain, mine))
        gain_parts = [gain, flipped(gain, 0, 1)]
    else:
        gain_parts = [lax.psum(gain_part, ("seq", "dp"))]
    other = flipped(mine, 0, 1)
    key_grad, value_grad = call(
        functools.partial(last_body, heads, dim, last), [(rows, BF16), (rows, BF16)],
        "vvvvv" + "v" * len(sums), flops=2 * matrix, moved=3 << 20,
    )(number, key, value, key_part, value_part, *sums)
    scale = 1.0 / math.sqrt(size * lax.axis_size("dp") * tokens)
    layer_out, gain_grad = call(
        functools.partial(layer_body, scale), [((half, model), BF16), (small, F32)],
        "vvvvv" + "v" * len(gain_parts), flops=2 * layer, moved=6 << 20,
    )(keep, w, took, mine, other, *gain_parts)
    return layer_out[None], query_grad[None], key_grad[None], value_grad[None], gain_grad


def solution(mesh):
    rows = P("dp", "seq", "head")
    return jax.shard_map(
        on_device,
        mesh=mesh,
        in_specs=(rows, rows, rows, P("dp", "seq"), P("head", None), P("head", None), P("dp", "seq", None)),
        out_specs=(P("dp", ("seq", "head"), None), rows, rows, rows, P("head", None)),
        check_vma=False,
    )
```

```python
import functools
import math

import jax
import jax.numpy as jnp
from jax import lax
from jax.experimental import pallas as pl
from jax.experimental.pallas import tpu as pltpu
from jax.sharding import PartitionSpec as P

EPSILON = 1e-05
F32 = jnp.float32
BF16 = jnp.bfloat16
TAIL = 16
GAIN = 4
PARTS = 2


def nn(a, b):
    return lax.dot_general(a, b, (((1,), (0,)), ((), ())), preferred_element_type=F32)


def nt(a, b):
    return lax.dot_general(a, b, (((1,), (1,)), ((), ())), preferred_element_type=F32)


def tn(a, b):
    return lax.dot_general(a, b, (((0,), (0,)), ((), ())), preferred_element_type=F32)


def call(body, outs, places, flops, moved, scratch=()):
    space = {"a": pl.ANY, "v": pltpu.VMEM, "h": pltpu.HBM}
    return pl.pallas_call(
        body,
        out_shape=[jax.ShapeDtypeStruct(s, t) for s, t in outs],
        in_specs=[pl.BlockSpec(memory_space=space[p]) for p in places],
        out_specs=[pl.BlockSpec(memory_space=pltpu.VMEM) for _ in outs],
        scratch_shapes=list(scratch),
        name=getattr(body, "func", body).__name__,
        cost_estimate=pl.CostEstimate(flops=flops, bytes_accessed=moved, transcendentals=0),
        compiler_params=pltpu.CompilerParams(vmem_limit_bytes=40 << 20),
    )


def pairing(size, pairs):
    partner = {i: (j, False) for a, b in pairs for i, j in ((a, b), (b, a))}
    route = []
    for i in range(size):
        to, same_stretch = partner.get(i, (i, True))
        route += [(2 * i + core, 2 * to + (core ^ same_stretch)) for core in (0, 1)]
    return route


def exchange(block, pairs):
    return lax.ppermute(block, ("seq", "dp"), pairing(lax.axis_size("seq"), pairs))


def blocks(size, distance, odd):
    return [(i, i + distance) for i in range(size - distance) if (i // distance) % 2 == odd]


def swaps(block, distance):
    size = lax.axis_size("seq")
    return [exchange(block, blocks(size, distance, odd)) for odd in (0, 1)]


def flipped(block, distance, cores):
    route = [
        (2 * i + core, 2 * (i ^ distance) + (core ^ cores))
        for i in range(lax.axis_size("seq"))
        for core in (0, 1)
    ]
    return lax.ppermute(block, ("seq", "dp"), route)


def put_tail(msg_ref, number, gain=None):
    rows, dim = msg_ref.shape[0] - TAIL, msg_ref.shape[1]
    high = jnp.zeros((GAIN, dim), F32) if gain is None else gain.astype(BF16).astype(F32)
    low = jnp.zeros((GAIN, dim), F32) if gain is None else gain - high
    low = low.astype(BF16).astype(F32)
    number = jnp.broadcast_to(number, (TAIL - 2 * GAIN, dim))
    msg_ref[rows:, :] = jnp.concatenate([high, low, number], axis=0).astype(BF16)
    return high + low


def sent_gain(msg_ref):
    tail = msg_ref[msg_ref.shape[0] - TAIL :, :].astype(F32)
    return tail[:GAIN, :] + tail[GAIN : 2 * GAIN, :]


def opened(msg):
    msg = msg.astype(F32)
    rows = msg.shape[0] - TAIL
    return msg[:rows, :], msg[rows + 2 * GAIN : rows + 2 * GAIN + 1, :]


def taken(even_ref, odd_ref, number, distance, forward):
    me, size = lax.axis_index("seq"), lax.axis_size("seq")
    upper = lax.rem(lax.div(me, distance), 2)
    from_odd = upper == 0 if forward else upper == 1
    there = me >= distance if forward else me + distance < size
    sums, theirs = opened(jnp.where(from_odd, odd_ref[...], even_ref[...]))
    return jnp.where(theirs == jnp.where(there, number, -1.0), sums, 0.0)


def beside(pair_ref, far_ref, number, forward):
    me, size = lax.axis_index("seq"), lax.axis_size("seq")
    in_pair = lax.rem(me, 2) == (1 if forward else 0)
    there = in_pair | (me >= 3 if forward else me + 3 < size)
    sums, theirs = opened(jnp.where(in_pair, pair_ref[...], far_ref[...]))
    return jnp.where(theirs == jnp.where(there, number, -1.0), sums, 0.0)


def total(refs, number, distance, forward):
    *near, even_ref, odd_ref = refs
    if len(near) == 1:
        first = near[0][...]
    else:
        first = beside(*near, number, forward)
    return first + taken(even_ref, odd_ref, number, distance, forward)


def opening_body(
    heads, dim, doc_any, key_hbm, value_hbm,
    key_ref, value_ref, number_ref, sum_ref, msg_ref, doc_ref, sems,
):
    copies = [
        pltpu.make_async_copy(src, dst, sems.at[i])
        for i, (src, dst) in enumerate(((key_hbm, key_ref), (value_hbm, value_ref), (doc_any, doc_ref)))
    ]
    for copy in copies:
        copy.start()
    copies[2].wait()
    number = jnp.full(number_ref.shape, doc_ref[0, 0] + 1, jnp.int32).astype(F32)
    number_ref[...] = number
    put_tail(msg_ref, number[:1, :])
    copies[0].wait()
    copies[1].wait()
    for h in range(heads):
        cols, rows = slice(h * dim, (h + 1) * dim), slice(h * dim, (h + 1) * dim)
        sums = tn(key_ref[:, cols], value_ref[:, cols])
        sum_ref[rows, :] = sums
        msg_ref[rows, :] = sums.astype(BF16)


def local_body(
    heads, dim, query_hbm, key_ref, value_ref, cot_hbm, w_hbm,
    query_ref, w_ref, weight_ref, within_ref, normed_grad_ref, cot_ref, sems,
):
    copies = [
        pltpu.make_async_copy(src, dst, sems.at[i])
        for i, (src, dst) in enumerate(((query_hbm, query_ref), (cot_hbm, cot_ref), (w_hbm, w_ref)))
    ]
    for copy in copies:
        copy.start()
    tokens = query_ref.shape[0]
    causal = lax.broadcasted_iota(jnp.int32, (tokens, tokens), 0) >= lax.broadcasted_iota(
        jnp.int32, (tokens, tokens), 1
    )
    copies[0].wait()
    for h in range(heads):
        cols = slice(h * dim, (h + 1) * dim)
        scores = nt(query_ref[:, cols], key_ref[:, cols])
        weights = jnp.where(causal, scores, 0.0).astype(BF16)
        weight_ref[h * tokens : (h + 1) * tokens, :] = weights
        within_ref[:, cols] = nn(weights, value_ref[:, cols])
    copies[1].wait()
    copies[2].wait()
    normed_grad_ref[...] = nt(cot_ref[...], w_ref[...])


def merge_gain(gains, own_ref, other_ref):
    return sent_gain(own_ref) + sent_gain(other_ref) if gains else None


def pair_body(forward, gains, number_ref, sum_ref, own_ref, pair_ref, msg_ref):
    rows = sum_ref.shape[0]
    number = number_ref[:1, :]
    leads = lax.rem(lax.axis_index("seq"), 2) == (1 if forward else 0)
    sums, theirs = opened(pair_ref[...])
    mine = sum_ref[...]
    same = theirs == number
    keep_mine, keep_theirs = same | leads, same | jnp.logical_not(leads)
    msg_ref[:rows, :] = (jnp.where(keep_mine, mine, 0.0) + jnp.where(keep_theirs, sums, 0.0)).astype(BF16)
    put_tail(msg_ref, jnp.where(leads, number, theirs), merge_gain(gains, own_ref, pair_ref))


def merge_body(distance, forward, gains, number_ref, sum_ref, own_ref, *refs):
    *term_ref, even_ref, odd_ref, out_ref, msg_ref = refs
    rows = sum_ref.shape[0]
    number = number_ref[:1, :]
    term = taken(even_ref, odd_ref, number, distance, forward)
    if term_ref:
        term = term + term_ref[0][...]
    out_ref[...] = term
    msg_ref[:rows, :] = (sum_ref[...] + term).astype(BF16)
    put_tail(msg_ref, number, merge_gain(gains, own_ref, even_ref))


def gain_body(own_ref, other_ref, out_ref):
    out_ref[...] = merge_gain(True, own_ref, other_ref)


def forward_body(
    heads, dim, distance, number_ref, query_ref, within_ref, normed_grad_ref, gain_ref, w_ref, *refs
):
    *sum_refs, state_ref, keep_ref = refs[: -5 - PARTS]
    send_refs = refs[-5 - PARTS : -5]
    grad_ref, outer_ref, msg_ref, gain_grad_ref, normed_ref = refs[-5:]
    half = keep_ref.shape[0]
    number = number_ref[:1, :]
    state_ref[...] = total(sum_refs, number, distance, True).astype(BF16)
    for h in range(heads):
        cols, rows = slice(h * dim, (h + 1) * dim), slice(h * dim, (h + 1) * dim)
        query = query_ref[:, cols]
        attended = within_ref[:, cols] + nn(query, state_ref[rows, :])
        inv_rms = lax.rsqrt(jnp.mean(attended * attended, axis=-1, keepdims=True) + EPSILON)
        unit = attended * inv_rms
        gain = gain_ref[h : h + 1, :]
        normed_ref[:, cols] = (unit * gain).astype(BF16)
        normed_grad = normed_grad_ref[:, cols]
        gain_grad_ref[h : h + 1, :] = jnp.sum(normed_grad * unit, axis=0, keepdims=True)
        scaled = normed_grad * gain
        grad = inv_rms * (scaled - unit * jnp.mean(scaled * unit, axis=-1, keepdims=True))
        grad = grad.astype(BF16)
        grad_ref[:, cols] = grad
        outer = tn(query, grad)
        outer_ref[rows, :] = outer
        msg_ref[rows, :] = outer.astype(BF16)
    put_tail(msg_ref, number, gain_grad_ref[...])
    head = lax.axis_index("head")
    keep_ref[...] = normed_ref[pl.ds(pl.multiple_of(head * half, half), half), :]
    give = normed_ref[pl.ds(pl.multiple_of((1 - head) * half, half), half), :]
    width = send_refs[0].shape[1]
    for i, send_ref in enumerate(send_refs):
        send_ref[...] = nn(give, w_ref[:, i * width : (i + 1) * width]).astype(BF16)


def backward_body(
    heads, dim, query_ref, key_ref, value_ref, weight_ref, grad_ref, state_ref, keep_ref, w_ref,
    query_grad_ref, key_part_ref, value_part_ref, own_ref,
):
    own_ref[...] = nn(keep_ref[...], w_ref[...])
    tokens = query_ref.shape[0]
    causal = lax.broadcasted_iota(jnp.int32, (tokens, tokens), 0) >= lax.broadcasted_iota(
        jnp.int32, (tokens, tokens), 1
    )
    for h in range(heads):
        cols, rows = slice(h * dim, (h + 1) * dim), slice(h * dim, (h + 1) * dim)
        grad = grad_ref[:, cols]
        grad_scores = nt(grad, value_ref[:, cols])
        grad_weights = jnp.where(causal, grad_scores, 0.0).astype(BF16)
        query_grad_ref[:, cols] = (
            nn(grad_weights, key_ref[:, cols]) + nt(grad, state_ref[rows, :])
        ).astype(BF16)
        key_part_ref[:, cols] = tn(grad_weights, query_ref[:, cols])
        value_part_ref[:, cols] = tn(weight_ref[h * tokens : (h + 1) * tokens, :], grad)


def last_body(
    heads, dim, distance, number_ref, key_ref, value_ref, key_part_ref, value_part_ref, *refs
):
    *sum_refs, key_grad_ref, value_grad_ref = refs
    state = total(sum_refs, number_ref[:1, :], distance, False).astype(BF16)
    for h in range(heads):
        cols, rows = slice(h * dim, (h + 1) * dim), slice(h * dim, (h + 1) * dim)
        key_grad_ref[:, cols] = (
            key_part_ref[:, cols] + nt(value_ref[:, cols], state[rows, :])
        ).astype(BF16)
        value_grad_ref[:, cols] = (
            value_part_ref[:, cols] + nn(key_ref[:, cols], state[rows, :])
        ).astype(BF16)


def layer_body(own_ref, *refs):
    *got_refs, out_ref = refs
    width = got_refs[0].shape[1]
    for i, got_ref in enumerate(got_refs):
        at = slice(i * width, (i + 1) * width)
        out_ref[:, at] = (own_ref[:, at] + got_ref[...].astype(F32)).astype(BF16)


def add_body(scale, one_ref, other_ref, out_ref):
    out_ref[...] = (one_ref[...] + other_ref[...]) * scale


def on_device(queries, key_rows, value_rows, stretch_doc, head_gain, w_out, cotangent):
    tokens, width = queries.shape[1:]
    heads, dim = head_gain.shape
    model = w_out.shape[1]
    size = lax.axis_size("seq")
    matrix = 2 * tokens * dim * dim * heads
    square = 2 * tokens * tokens * dim * heads
    layer = tokens * width * model
    rows, summed, message = (tokens, width), (heads * dim, dim), (heads * dim + TAIL, dim)
    small, half = (heads, dim), (tokens // 2, model)
    distances = [1]
    while 2 * distances[-1] - 1 < size // 2 - 1:
        distances.append(2 * distances[-1])
    last = distances[-1]
    gains = size & (size - 1) == 0 and len(distances) > 1

    beside = []

    def spread(outer, msg, forward):
        carry = gains and not forward
        if last == 2:
            pair = exchange(msg, blocks(size, 1, 0))
            pair, beside[0] = lax.optimization_barrier((pair, beside[0]))
            far = exchange(msg, [(i, i + 3) for i in range(1, size - 3, 2)])
            (msg,) = call(
                functools.partial(pair_body, forward, carry), [(message, BF16)], "vvvv", flops=0, moved=1 << 20
            )(number, outer, msg, pair)
            even, odd = swaps(msg, last)
            even, far = lax.optimization_barrier((even, far))
            return [pair, far, even, odd], msg
        terms = []
        for distance in distances[:-1]:
            even, odd = swaps(msg, distance)
            *terms, msg = call(
                functools.partial(merge_body, distance, forward, carry), [(summed, F32), (message, BF16)],
                "vvvvv" + "v" * len(terms), flops=0, moved=1 << 20,
            )(number, outer, msg, *terms, even, odd)
        return [*terms, *swaps(msg, last)], msg

    in_hbm = lambda block: pltpu.with_memory_space_constraint(block, pltpu.HBM)
    key, value, number, outer, msg = call(
        functools.partial(opening_body, heads, dim),
        [(rows, BF16)] * 2 + [((8, dim), F32), (summed, F32), (message, BF16)],
        "ahh", flops=matrix, moved=1 << 20, scratch=[pltpu.SMEM((1, 1), jnp.int32), pltpu.SemaphoreType.DMA((3,))],
    )(stretch_doc, in_hbm(key_rows[0]), in_hbm(value_rows[0]))
    query, w, weights, within, normed_grad = call(
        functools.partial(local_body, heads, dim),
        [(rows, BF16), ((width, model), BF16), ((heads * tokens, tokens), BF16), (rows, F32), (rows, F32)],
        "hvvhh", flops=2 * square + 2 * layer, moved=6 << 20,
        scratch=[pltpu.VMEM((tokens, model), BF16), pltpu.SemaphoreType.DMA((3,))],
    )(in_hbm(queries[0]), key, value, in_hbm(cotangent[0]), in_hbm(w_out))
    beside.append(within)
    sums, _ = spread(outer, msg, True)
    (within,) = beside
    state, keep, *send, grad, outer, msg, gain_part = call(
        functools.partial(forward_body, heads, dim, last),
        [
            (summed, BF16), ((tokens // 2, width), BF16), *[((tokens // 2, model // PARTS), BF16)] * PARTS,
            (rows, BF16), (summed, F32), (message, BF16), (small, F32),
        ],
        "vvvvvv" + "v" * len(sums), flops=2 * matrix + layer, moved=4 << 20, scratch=[pltpu.VMEM(rows, BF16)],
    )(number, query, within, normed_grad, head_gain, w, *sums)
    got = [lax.ppermute(part, "head", [(0, 1), (1, 0)]) for part in send]
    query_grad, key_part, value_part, own = call(
        functools.partial(backward_body, heads, dim),
        [(rows, BF16), (rows, F32), (rows, F32), (half, F32)],
        "vvvvvvvv", flops=0, moved=1 << 16,
    )(query, key, value, weights, grad, state, keep, w)
    beside[0] = key_part
    sums, msg = spread(outer, msg, False)
    (key_part,) = beside
    scale = 1.0 / math.sqrt(size * lax.axis_size("dp") * tokens)
    add = lambda scale, *gain: call(
        functools.partial(add_body, scale), [(small, F32)], "vv", flops=0, moved=1 << 16
    )(*gain)[0]
    if gains:
        (gain,) = call(gain_body, [(small, F32)], "vv", flops=0, moved=1 << 16)(msg, sums[-2])
        far = flipped(gain, size // 2, 0)
    key_grad, value_grad = call(
        functools.partial(last_body, heads, dim, last), [(rows, BF16), (rows, BF16)],
        "vvvvv" + "v" * len(sums), flops=2 * matrix, moved=3 << 20,
    )(number, key, value, key_part, value_part, *sums)
    if gains:
        far, key_grad = lax.optimization_barrier((far, key_grad))
        gain = add(1.0, gain, far)
        gain_grad = add(scale, gain, flipped(gain, 0, 1))
    else:
        gain_grad = lax.psum(gain_part, ("seq", "dp")) * scale
    (layer_out,) = call(layer_body, [(half, BF16)], "v" + "v" * PARTS, flops=0, moved=2 << 20)(own, *got)
    return layer_out[None], query_grad[None], key_grad[None], value_grad[None], gain_grad


def solution(mesh):
    rows = P("dp", "seq", "head")
    return jax.shard_map(
        on_device,
        mesh=mesh,
        in_specs=(rows, rows, rows, P("dp", "seq"), P("head", None), P("head", None), P("dp", "seq", None)),
        out_specs=(P("dp", ("seq", "head"), None), rows, rows, rows, P("head", None)),
        check_vma=False,
    )
```

```python
import functools
import math

import jax
import jax.numpy as jnp
from jax import lax
from jax.experimental import pallas as pl
from jax.experimental.pallas import tpu as pltpu
from jax.sharding import PartitionSpec as P

EPSILON = 1e-05
F32 = jnp.float32
BF16 = jnp.bfloat16
TAIL = 16
TIE = (True, True)
GAIN = 4
PARTS = 1


def nn(a, b):
    return lax.dot_general(a, b, (((1,), (0,)), ((), ())), preferred_element_type=F32)


def nt(a, b):
    return lax.dot_general(a, b, (((1,), (1,)), ((), ())), preferred_element_type=F32)


def tn(a, b):
    return lax.dot_general(a, b, (((0,), (0,)), ((), ())), preferred_element_type=F32)


def call(body, outs, places, flops, moved, scratch=()):
    space = {"a": pl.ANY, "v": pltpu.VMEM, "h": pltpu.HBM}
    return pl.pallas_call(
        body,
        out_shape=[jax.ShapeDtypeStruct(s, t) for s, t in outs],
        in_specs=[pl.BlockSpec(memory_space=space[p]) for p in places],
        out_specs=[pl.BlockSpec(memory_space=pltpu.VMEM) for _ in outs],
        scratch_shapes=list(scratch),
        name=getattr(body, "func", body).__name__,
        cost_estimate=pl.CostEstimate(flops=flops, bytes_accessed=moved, transcendentals=0),
        compiler_params=pltpu.CompilerParams(vmem_limit_bytes=40 << 20),
    )


def pairing(size, pairs):
    partner = {i: (j, False) for a, b in pairs for i, j in ((a, b), (b, a))}
    route = []
    for i in range(size):
        to, same_stretch = partner.get(i, (i, True))
        route += [(2 * i + core, 2 * to + (core ^ same_stretch)) for core in (0, 1)]
    return route


def exchange(block, pairs):
    return lax.ppermute(block, ("seq", "dp"), pairing(lax.axis_size("seq"), pairs))


def blocks(size, distance, odd):
    return [(i, i + distance) for i in range(size - distance) if (i // distance) % 2 == odd]


def swaps(block, distance):
    size = lax.axis_size("seq")
    return [exchange(block, blocks(size, distance, odd)) for odd in (0, 1)]


def flipped(block, distance, cores):
    route = [
        (2 * i + core, 2 * (i ^ distance) + (core ^ cores))
        for i in range(lax.axis_size("seq"))
        for core in (0, 1)
    ]
    return lax.ppermute(block, ("seq", "dp"), route)


def put_tail(msg_ref, number, gain=None):
    rows, dim = msg_ref.shape[0] - TAIL, msg_ref.shape[1]
    high = jnp.zeros((GAIN, dim), F32) if gain is None else gain.astype(BF16).astype(F32)
    low = jnp.zeros((GAIN, dim), F32) if gain is None else gain - high
    low = low.astype(BF16).astype(F32)
    number = jnp.broadcast_to(number, (TAIL - 2 * GAIN, dim))
    msg_ref[rows:, :] = jnp.concatenate([high, low, number], axis=0).astype(BF16)
    return high + low


def sent_gain(msg_ref):
    tail = msg_ref[msg_ref.shape[0] - TAIL :, :].astype(F32)
    return tail[:GAIN, :] + tail[GAIN : 2 * GAIN, :]


def opened(msg):
    msg = msg.astype(F32)
    rows = msg.shape[0] - TAIL
    return msg[:rows, :], msg[rows + 2 * GAIN : rows + 2 * GAIN + 1, :]


def taken(even_ref, odd_ref, number, distance, forward):
    me, size = lax.axis_index("seq"), lax.axis_size("seq")
    upper = lax.rem(lax.div(me, distance), 2)
    from_odd = upper == 0 if forward else upper == 1
    there = me >= distance if forward else me + distance < size
    sums, theirs = opened(jnp.where(from_odd, odd_ref[...], even_ref[...]))
    return jnp.where(theirs == jnp.where(there, number, -1.0), sums, 0.0)


def beside(pair_ref, far_ref, number, forward):
    me, size = lax.axis_index("seq"), lax.axis_size("seq")
    in_pair = lax.rem(me, 2) == (1 if forward else 0)
    there = in_pair | (me >= 3 if forward else me + 3 < size)
    sums, theirs = opened(jnp.where(in_pair, pair_ref[...], far_ref[...]))
    return jnp.where(theirs == jnp.where(there, number, -1.0), sums, 0.0)


def total(refs, number, distance, forward):
    *near, even_ref, odd_ref = refs
    if len(near) == 1:
        first = near[0][...]
    else:
        first = beside(*near, number, forward)
    return first + taken(even_ref, odd_ref, number, distance, forward)


def opening_body(
    heads, dim, doc_any, key_hbm, value_hbm,
    key_ref, value_ref, number_ref, sum_ref, msg_ref, doc_ref, sems,
):
    copies = [
        pltpu.make_async_copy(src, dst, sems.at[i])
        for i, (src, dst) in enumerate(((key_hbm, key_ref), (value_hbm, value_ref), (doc_any, doc_ref)))
    ]
    for copy in copies:
        copy.start()
    copies[2].wait()
    number = jnp.full(number_ref.shape, doc_ref[0, 0] + 1, jnp.int32).astype(F32)
    number_ref[...] = number
    put_tail(msg_ref, number[:1, :])
    copies[0].wait()
    copies[1].wait()
    for h in range(heads):
        cols, rows = slice(h * dim, (h + 1) * dim), slice(h * dim, (h + 1) * dim)
        sums = tn(key_ref[:, cols], value_ref[:, cols])
        sum_ref[rows, :] = sums
        msg_ref[rows, :] = sums.astype(BF16)


def local_body(
    heads, dim, query_hbm, key_ref, value_ref, cot_hbm, w_hbm,
    query_ref, w_ref, weight_ref, within_ref, normed_grad_ref, cot_ref, sems,
):
    copies = [
        pltpu.make_async_copy(src, dst, sems.at[i])
        for i, (src, dst) in enumerate(((query_hbm, query_ref), (cot_hbm, cot_ref), (w_hbm, w_ref)))
    ]
    for copy in copies:
        copy.start()
    tokens = query_ref.shape[0]
    causal = lax.broadcasted_iota(jnp.int32, (tokens, tokens), 0) >= lax.broadcasted_iota(
        jnp.int32, (tokens, tokens), 1
    )
    copies[0].wait()
    for h in range(heads):
        cols = slice(h * dim, (h + 1) * dim)
        scores = nt(query_ref[:, cols], key_ref[:, cols])
        weights = jnp.where(causal, scores, 0.0).astype(BF16)
        weight_ref[h * tokens : (h + 1) * tokens, :] = weights
        within_ref[:, cols] = nn(weights, value_ref[:, cols])
    copies[1].wait()
    copies[2].wait()
    normed_grad_ref[...] = nt(cot_ref[...], w_ref[...])


def merge_gain(gains, own_ref, other_ref):
    return sent_gain(own_ref) + sent_gain(other_ref) if gains else None


def pair_body(forward, gains, number_ref, sum_ref, own_ref, pair_ref, *refs):
    *gain_refs, msg_ref = refs
    rows = sum_ref.shape[0]
    number = number_ref[:1, :]
    leads = lax.rem(lax.axis_index("seq"), 2) == (1 if forward else 0)
    sums, theirs = opened(pair_ref[...])
    mine = sum_ref[...]
    same = theirs == number
    keep_mine, keep_theirs = same | leads, same | jnp.logical_not(leads)
    msg_ref[:rows, :] = (jnp.where(keep_mine, mine, 0.0) + jnp.where(keep_theirs, sums, 0.0)).astype(BF16)
    gain = merge_gain(gains, own_ref, pair_ref)
    if gains:
        gain = gain + (gain_refs[0][...] + gain_refs[1][...])
    put_tail(msg_ref, jnp.where(leads, number, theirs), gain)


def merge_body(distance, forward, gains, number_ref, sum_ref, own_ref, *refs):
    *term_ref, even_ref, odd_ref, out_ref, msg_ref = refs
    rows = sum_ref.shape[0]
    number = number_ref[:1, :]
    term = taken(even_ref, odd_ref, number, distance, forward)
    if term_ref:
        term = term + term_ref[0][...]
    out_ref[...] = term
    msg_ref[:rows, :] = (sum_ref[...] + term).astype(BF16)
    put_tail(msg_ref, number, merge_gain(gains, own_ref, even_ref))


def gain_body(own_ref, other_ref, out_ref):
    out_ref[...] = merge_gain(True, own_ref, other_ref)


def forward_body(
    heads, dim, distance, number_ref, query_ref, within_ref, normed_grad_ref, gain_ref, w_ref, *refs
):
    *sum_refs, state_ref, keep_ref = refs[: -5 - PARTS]
    send_refs = refs[-5 - PARTS : -5]
    grad_ref, outer_ref, msg_ref, gain_grad_ref, normed_ref = refs[-5:]
    half = keep_ref.shape[0]
    number = number_ref[:1, :]
    state_ref[...] = total(sum_refs, number, distance, True).astype(BF16)
    for h in range(heads):
        cols, rows = slice(h * dim, (h + 1) * dim), slice(h * dim, (h + 1) * dim)
        query = query_ref[:, cols]
        attended = within_ref[:, cols] + nn(query, state_ref[rows, :])
        inv_rms = lax.rsqrt(jnp.mean(attended * attended, axis=-1, keepdims=True) + EPSILON)
        unit = attended * inv_rms
        gain = gain_ref[h : h + 1, :]
        normed_ref[:, cols] = (unit * gain).astype(BF16)
        normed_grad = normed_grad_ref[:, cols]
        gain_grad_ref[h : h + 1, :] = jnp.sum(normed_grad * unit, axis=0, keepdims=True)
        scaled = normed_grad * gain
        grad = inv_rms * (scaled - unit * jnp.mean(scaled * unit, axis=-1, keepdims=True))
        grad = grad.astype(BF16)
        grad_ref[:, cols] = grad
        outer = tn(query, grad)
        outer_ref[rows, :] = outer
        msg_ref[rows, :] = outer.astype(BF16)
    gain_grad_ref[...] = put_tail(msg_ref, number, gain_grad_ref[...])
    head = lax.axis_index("head")
    keep_ref[...] = normed_ref[pl.ds(pl.multiple_of(head * half, half), half), :]
    give = normed_ref[pl.ds(pl.multiple_of((1 - head) * half, half), half), :]
    width = send_refs[0].shape[1]
    for i, send_ref in enumerate(send_refs):
        send_ref[...] = nn(give, w_ref[:, i * width : (i + 1) * width]).astype(BF16)


def backward_body(
    heads, dim, query_ref, key_ref, value_ref, weight_ref, grad_ref, state_ref, keep_ref, w_ref,
    query_grad_ref, key_part_ref, value_part_ref, own_ref,
):
    own_ref[...] = nn(keep_ref[...], w_ref[...])
    tokens = query_ref.shape[0]
    causal = lax.broadcasted_iota(jnp.int32, (tokens, tokens), 0) >= lax.broadcasted_iota(
        jnp.int32, (tokens, tokens), 1
    )
    for h in range(heads):
        cols, rows = slice(h * dim, (h + 1) * dim), slice(h * dim, (h + 1) * dim)
        grad = grad_ref[:, cols]
        grad_scores = nt(grad, value_ref[:, cols])
        grad_weights = jnp.where(causal, grad_scores, 0.0).astype(BF16)
        query_grad_ref[:, cols] = (
            nn(grad_weights, key_ref[:, cols]) + nt(grad, state_ref[rows, :])
        ).astype(BF16)
        key_part_ref[:, cols] = tn(grad_weights, query_ref[:, cols])
        value_part_ref[:, cols] = tn(weight_ref[h * tokens : (h + 1) * tokens, :], grad)


def last_body(
    heads, dim, distance, number_ref, key_ref, value_ref, key_part_ref, value_part_ref, *refs
):
    *sum_refs, key_grad_ref, value_grad_ref = refs
    state = total(sum_refs, number_ref[:1, :], distance, False).astype(BF16)
    for h in range(heads):
        cols, rows = slice(h * dim, (h + 1) * dim), slice(h * dim, (h + 1) * dim)
        key_grad_ref[:, cols] = (
            key_part_ref[:, cols] + nt(value_ref[:, cols], state[rows, :])
        ).astype(BF16)
        value_grad_ref[:, cols] = (
            value_part_ref[:, cols] + nn(key_ref[:, cols], state[rows, :])
        ).astype(BF16)


def layer_body(scale, own_ref, *refs):
    got_refs, gain_refs = refs[:PARTS], refs[PARTS:-2]
    out_ref, gain_grad_ref = refs[-2:]
    width = got_refs[0].shape[1]
    for i, got_ref in enumerate(got_refs):
        at = slice(i * width, (i + 1) * width)
        out_ref[:, at] = (own_ref[:, at] + got_ref[...].astype(F32)).astype(BF16)
    gain = gain_refs[0][...]
    if len(gain_refs) > 1:
        gain = gain + gain_refs[1][...]
    gain_grad_ref[...] = gain * scale


def on_device(queries, key_rows, value_rows, stretch_doc, head_gain, w_out, cotangent):
    tokens, width = queries.shape[1:]
    heads, dim = head_gain.shape
    model = w_out.shape[1]
    size = lax.axis_size("seq")
    matrix = 2 * tokens * dim * dim * heads
    square = 2 * tokens * tokens * dim * heads
    layer = tokens * width * model
    rows, summed, message = (tokens, width), (heads * dim, dim), (heads * dim + TAIL, dim)
    small, half = (heads, dim), (tokens // 2, model)
    distances = [1]
    while 2 * distances[-1] - 1 < size // 2 - 1:
        distances.append(2 * distances[-1])
    last = distances[-1]
    gains = size == 8

    beside = []

    def spread(outer, msg, forward, gain_part=None):
        carry = gain_part is not None
        if last == 2:
            pair = exchange(msg, blocks(size, 1, 0))
            far = exchange(msg, [(i, i + 3) for i in range(1, size - 3, 2)])
            gain = [flipped(gain_part, to, 0) for to in (size // 2, size // 2 + 1)] if carry else []
            if TIE[0] and forward or TIE[1] and not forward:
                pair, beside[0] = lax.optimization_barrier((pair, beside[0]))
            (msg,) = call(
                functools.partial(pair_body, forward, carry), [(message, BF16)], "vvvv" + "v" * len(gain), flops=0, moved=1 << 20
            )(number, outer, msg, pair, *gain)
            even, odd = swaps(msg, last)
            even, far = lax.optimization_barrier((even, far))
            return [pair, far, even, odd], msg
        terms = []
        for distance in distances[:-1]:
            even, odd = swaps(msg, distance)
            *terms, msg = call(
                functools.partial(merge_body, distance, forward, carry), [(summed, F32), (message, BF16)],
                "vvvvv" + "v" * len(terms), flops=0, moved=1 << 20,
            )(number, outer, msg, *terms, even, odd)
        return [*terms, *swaps(msg, last)], msg

    in_hbm = lambda block: pltpu.with_memory_space_constraint(block, pltpu.HBM)
    key, value, number, outer, msg = call(
        functools.partial(opening_body, heads, dim),
        [(rows, BF16)] * 2 + [((8, dim), F32), (summed, F32), (message, BF16)],
        "ahh", flops=matrix, moved=1 << 20, scratch=[pltpu.SMEM((1, 1), jnp.int32), pltpu.SemaphoreType.DMA((3,))],
    )(stretch_doc, in_hbm(key_rows[0]), in_hbm(value_rows[0]))
    query, w, weights, within, normed_grad = call(
        functools.partial(local_body, heads, dim),
        [(rows, BF16), ((width, model), BF16), ((heads * tokens, tokens), BF16), (rows, F32), (rows, F32)],
        "hvvhh", flops=2 * square + 2 * layer, moved=6 << 20,
        scratch=[pltpu.VMEM((tokens, model), BF16), pltpu.SemaphoreType.DMA((3,))],
    )(in_hbm(queries[0]), key, value, in_hbm(cotangent[0]), in_hbm(w_out))
    beside.append(within)
    sums, _ = spread(outer, msg, True)
    (within,) = beside
    state, keep, *send, grad, outer, msg, gain_part = call(
        functools.partial(forward_body, heads, dim, last),
        [
            (summed, BF16), ((tokens // 2, width), BF16), *[((tokens // 2, model // PARTS), BF16)] * PARTS,
            (rows, BF16), (summed, F32), (message, BF16), (small, F32),
        ],
        "vvvvvv" + "v" * len(sums), flops=2 * matrix + layer, moved=4 << 20, scratch=[pltpu.VMEM(rows, BF16)],
    )(number, query, within, normed_grad, head_gain, w, *sums)
    got = [lax.ppermute(part, "head", [(0, 1), (1, 0)]) for part in send]
    query_grad, key_part, value_part, own = call(
        functools.partial(backward_body, heads, dim),
        [(rows, BF16), (rows, F32), (rows, F32), (half, F32)],
        "vvvvvvvv", flops=0, moved=1 << 16,
    )(query, key, value, weights, grad, state, keep, w)
    beside[0] = key_part
    sums, msg = spread(outer, msg, False, gain_part if gains else None)
    (key_part,) = beside
    scale = 1.0 / math.sqrt(size * lax.axis_size("dp") * tokens)
    if gains:
        (gain,) = call(gain_body, [(small, F32)], "vv", flops=0, moved=1 << 16)(msg, sums[-2])
        gain = [gain, flipped(gain, 0, 1)]
    else:
        gain = [lax.psum(gain_part, ("seq", "dp"))]
    key_grad, value_grad = call(
        functools.partial(last_body, heads, dim, last), [(rows, BF16), (rows, BF16)],
        "vvvvv" + "v" * len(sums), flops=2 * matrix, moved=3 << 20,
    )(number, key, value, key_part, value_part, *sums)
    layer_out, gain_grad = call(
        functools.partial(layer_body, scale), [(half, BF16), (small, F32)], "v" + "v" * (PARTS + len(gain)),
        flops=0, moved=2 << 20,
    )(own, *got, *gain)
    return layer_out[None], query_grad[None], key_grad[None], value_grad[None], gain_grad


def solution(mesh):
    rows = P("dp", "seq", "head")
    return jax.shard_map(
        on_device,
        mesh=mesh,
        in_specs=(rows, rows, rows, P("dp", "seq"), P("head", None), P("head", None), P("dp", "seq", None)),
        out_specs=(P("dp", ("seq", "head"), None), rows, rows, rows, P("head", None)),
        check_vma=False,
    )
```

```python
import functools
import math

import jax
import jax.numpy as jnp
from jax import lax
from jax.experimental import pallas as pl
from jax.experimental.pallas import tpu as pltpu
from jax.sharding import PartitionSpec as P

EPSILON = 1e-05
F32 = jnp.float32
BF16 = jnp.bfloat16
TAIL = 16
TIE = (True, True)
GAIN = 4
PARTS = 1


def nn(a, b):
    return lax.dot_general(a, b, (((1,), (0,)), ((), ())), preferred_element_type=F32)


def nt(a, b):
    return lax.dot_general(a, b, (((1,), (1,)), ((), ())), preferred_element_type=F32)


def tn(a, b):
    return lax.dot_general(a, b, (((0,), (0,)), ((), ())), preferred_element_type=F32)


def call(body, outs, places, flops, moved, scratch=()):
    space = {"a": pl.ANY, "v": pltpu.VMEM, "h": pltpu.HBM}
    return pl.pallas_call(
        body,
        out_shape=[jax.ShapeDtypeStruct(s, t) for s, t in outs],
        in_specs=[pl.BlockSpec(memory_space=space[p]) for p in places],
        out_specs=[pl.BlockSpec(memory_space=pltpu.VMEM) for _ in outs],
        scratch_shapes=list(scratch),
        name=getattr(body, "func", body).__name__,
        cost_estimate=pl.CostEstimate(flops=flops, bytes_accessed=moved, transcendentals=0),
        compiler_params=pltpu.CompilerParams(vmem_limit_bytes=40 << 20),
    )


def pairing(size, pairs):
    partner = {i: (j, False) for a, b in pairs for i, j in ((a, b), (b, a))}
    route = []
    for i in range(size):
        to, same_stretch = partner.get(i, (i, True))
        route += [(2 * i + core, 2 * to + (core ^ same_stretch)) for core in (0, 1)]
    return route


def exchange(block, pairs):
    return lax.ppermute(block, ("seq", "dp"), pairing(lax.axis_size("seq"), pairs))


def blocks(size, distance, odd):
    return [(i, i + distance) for i in range(size - distance) if (i // distance) % 2 == odd]


def swaps(block, distance):
    size = lax.axis_size("seq")
    return [exchange(block, blocks(size, distance, odd)) for odd in (0, 1)]


def turned(block, distance):
    size = lax.axis_size("seq")
    return lax.ppermute(block, "seq", [(i, (i + distance) % size) for i in range(size)])


def flipped(block, distance, cores):
    route = [
        (2 * i + core, 2 * (i ^ distance) + (core ^ cores))
        for i in range(lax.axis_size("seq"))
        for core in (0, 1)
    ]
    return lax.ppermute(block, ("seq", "dp"), route)


def put_tail(msg_ref, number, gain=None):
    rows, dim = msg_ref.shape[0] - TAIL, msg_ref.shape[1]
    high = jnp.zeros((GAIN, dim), F32) if gain is None else gain.astype(BF16).astype(F32)
    low = jnp.zeros((GAIN, dim), F32) if gain is None else gain - high
    low = low.astype(BF16).astype(F32)
    number = jnp.broadcast_to(number, (TAIL - 2 * GAIN, dim))
    msg_ref[rows:, :] = jnp.concatenate([high, low, number], axis=0).astype(BF16)
    return high + low


def sent_gain(msg_ref):
    tail = msg_ref[msg_ref.shape[0] - TAIL :, :].astype(F32)
    return tail[:GAIN, :] + tail[GAIN : 2 * GAIN, :]


def opened(msg):
    msg = msg.astype(F32)
    rows = msg.shape[0] - TAIL
    return msg[:rows, :], msg[rows + 2 * GAIN : rows + 2 * GAIN + 1, :]


def taken(even_ref, odd_ref, number, distance, forward):
    me, size = lax.axis_index("seq"), lax.axis_size("seq")
    upper = lax.rem(lax.div(me, distance), 2)
    from_odd = upper == 0 if forward else upper == 1
    there = me >= distance if forward else me + distance < size
    sums, theirs = opened(jnp.where(from_odd, odd_ref[...], even_ref[...]))
    return jnp.where(theirs == jnp.where(there, number, -1.0), sums, 0.0)


def beside(pair_ref, far_ref, number, forward):
    me, size = lax.axis_index("seq"), lax.axis_size("seq")
    in_pair = lax.rem(me, 2) == (1 if forward else 0)
    there = in_pair | (me >= 3 if forward else me + 3 < size)
    sums, theirs = opened(jnp.where(in_pair, pair_ref[...], far_ref[...]))
    return jnp.where(theirs == jnp.where(there, number, -1.0), sums, 0.0)


def total(refs, number, distance, forward):
    *near, even_ref, odd_ref = refs
    if len(near) == 1:
        first = near[0][...]
    else:
        first = beside(*near, number, forward)
    return first + taken(even_ref, odd_ref, number, distance, forward)


def opening_body(
    heads, dim, doc_any, key_hbm, value_hbm,
    key_ref, value_ref, number_ref, sum_ref, msg_ref, doc_ref, sems,
):
    copies = [
        pltpu.make_async_copy(src, dst, sems.at[i])
        for i, (src, dst) in enumerate(((key_hbm, key_ref), (value_hbm, value_ref), (doc_any, doc_ref)))
    ]
    for copy in copies:
        copy.start()
    copies[2].wait()
    number = jnp.full(number_ref.shape, doc_ref[0, 0] + 1, jnp.int32).astype(F32)
    number_ref[...] = number
    put_tail(msg_ref, number[:1, :])
    copies[0].wait()
    copies[1].wait()
    for h in range(heads):
        cols, rows = slice(h * dim, (h + 1) * dim), slice(h * dim, (h + 1) * dim)
        sums = tn(key_ref[:, cols], value_ref[:, cols])
        sum_ref[rows, :] = sums
        msg_ref[rows, :] = sums.astype(BF16)


def local_body(
    heads, dim, query_hbm, key_ref, value_ref, cot_hbm, w_hbm,
    query_ref, w_ref, weight_ref, within_ref, normed_grad_ref, cot_ref, sems,
):
    copies = [
        pltpu.make_async_copy(src, dst, sems.at[i])
        for i, (src, dst) in enumerate(((query_hbm, query_ref), (cot_hbm, cot_ref), (w_hbm, w_ref)))
    ]
    for copy in copies:
        copy.start()
    tokens = query_ref.shape[0]
    causal = lax.broadcasted_iota(jnp.int32, (tokens, tokens), 0) >= lax.broadcasted_iota(
        jnp.int32, (tokens, tokens), 1
    )
    copies[0].wait()
    for h in range(heads):
        cols = slice(h * dim, (h + 1) * dim)
        scores = nt(query_ref[:, cols], key_ref[:, cols])
        weights = jnp.where(causal, scores, 0.0).astype(BF16)
        weight_ref[h * tokens : (h + 1) * tokens, :] = weights
        within_ref[:, cols] = nn(weights, value_ref[:, cols])
    copies[1].wait()
    copies[2].wait()
    normed_grad_ref[...] = nt(cot_ref[...], w_ref[...])


def merge_gain(gains, own_ref, other_ref):
    return sent_gain(own_ref) + sent_gain(other_ref) if gains else None


def pair_body(forward, gains, number_ref, sum_ref, own_ref, pair_ref, *refs):
    msg_ref, *gain_ref = refs
    rows = sum_ref.shape[0]
    number = number_ref[:1, :]
    leads = lax.rem(lax.axis_index("seq"), 2) == (1 if forward else 0)
    sums, theirs = opened(pair_ref[...])
    mine = sum_ref[...]
    same = theirs == number
    keep_mine, keep_theirs = same | leads, same | jnp.logical_not(leads)
    msg_ref[:rows, :] = (jnp.where(keep_mine, mine, 0.0) + jnp.where(keep_theirs, sums, 0.0)).astype(BF16)
    gain = put_tail(msg_ref, jnp.where(leads, number, theirs), merge_gain(gains, own_ref, pair_ref))
    if gains:
        gain_ref[0][...] = gain


def merge_body(distance, forward, gains, number_ref, sum_ref, own_ref, *refs):
    *term_ref, even_ref, odd_ref, out_ref, msg_ref = refs
    rows = sum_ref.shape[0]
    number = number_ref[:1, :]
    term = taken(even_ref, odd_ref, number, distance, forward)
    if term_ref:
        term = term + term_ref[0][...]
    out_ref[...] = term
    msg_ref[:rows, :] = (sum_ref[...] + term).astype(BF16)
    put_tail(msg_ref, number, merge_gain(gains, own_ref, even_ref))


def gain_body(own_ref, far_ref, farther_ref, near_ref, out_ref):
    out_ref[...] = (own_ref[...] + far_ref[...]) + (sent_gain(near_ref) + farther_ref[...])


def forward_body(
    heads, dim, distance, number_ref, query_ref, within_ref, normed_grad_ref, gain_ref, w_ref, *refs
):
    *sum_refs, state_ref, keep_ref = refs[: -5 - PARTS]
    send_refs = refs[-5 - PARTS : -5]
    grad_ref, outer_ref, msg_ref, gain_grad_ref, normed_ref = refs[-5:]
    half = keep_ref.shape[0]
    number = number_ref[:1, :]
    state_ref[...] = total(sum_refs, number, distance, True).astype(BF16)
    for h in range(heads):
        cols, rows = slice(h * dim, (h + 1) * dim), slice(h * dim, (h + 1) * dim)
        query = query_ref[:, cols]
        attended = within_ref[:, cols] + nn(query, state_ref[rows, :])
        inv_rms = lax.rsqrt(jnp.mean(attended * attended, axis=-1, keepdims=True) + EPSILON)
        unit = attended * inv_rms
        gain = gain_ref[h : h + 1, :]
        normed_ref[:, cols] = (unit * gain).astype(BF16)
        normed_grad = normed_grad_ref[:, cols]
        gain_grad_ref[h : h + 1, :] = jnp.sum(normed_grad * unit, axis=0, keepdims=True)
        scaled = normed_grad * gain
        grad = inv_rms * (scaled - unit * jnp.mean(scaled * unit, axis=-1, keepdims=True))
        grad = grad.astype(BF16)
        grad_ref[:, cols] = grad
        outer = tn(query, grad)
        outer_ref[rows, :] = outer
        msg_ref[rows, :] = outer.astype(BF16)
    gain_grad_ref[...] = put_tail(msg_ref, number, gain_grad_ref[...])
    head = lax.axis_index("head")
    keep_ref[...] = normed_ref[pl.ds(pl.multiple_of(head * half, half), half), :]
    give = normed_ref[pl.ds(pl.multiple_of((1 - head) * half, half), half), :]
    width = send_refs[0].shape[1]
    for i, send_ref in enumerate(send_refs):
        send_ref[...] = nn(give, w_ref[:, i * width : (i + 1) * width]).astype(BF16)


def backward_body(
    heads, dim, query_ref, key_ref, value_ref, weight_ref, grad_ref, state_ref, keep_ref, w_ref,
    query_grad_ref, key_part_ref, value_part_ref, own_ref,
):
    own_ref[...] = nn(keep_ref[...], w_ref[...])
    tokens = query_ref.shape[0]
    causal = lax.broadcasted_iota(jnp.int32, (tokens, tokens), 0) >= lax.broadcasted_iota(
        jnp.int32, (tokens, tokens), 1
    )
    for h in range(heads):
        cols, rows = slice(h * dim, (h + 1) * dim), slice(h * dim, (h + 1) * dim)
        grad = grad_ref[:, cols]
        grad_scores = nt(grad, value_ref[:, cols])
        grad_weights = jnp.where(causal, grad_scores, 0.0).astype(BF16)
        query_grad_ref[:, cols] = (
            nn(grad_weights, key_ref[:, cols]) + nt(grad, state_ref[rows, :])
        ).astype(BF16)
        key_part_ref[:, cols] = tn(grad_weights, query_ref[:, cols])
        value_part_ref[:, cols] = tn(weight_ref[h * tokens : (h + 1) * tokens, :], grad)


def last_body(
    heads, dim, distance, number_ref, key_ref, value_ref, key_part_ref, value_part_ref, *refs
):
    *sum_refs, key_grad_ref, value_grad_ref = refs
    state = total(sum_refs, number_ref[:1, :], distance, False).astype(BF16)
    for h in range(heads):
        cols, rows = slice(h * dim, (h + 1) * dim), slice(h * dim, (h + 1) * dim)
        key_grad_ref[:, cols] = (
            key_part_ref[:, cols] + nt(value_ref[:, cols], state[rows, :])
        ).astype(BF16)
        value_grad_ref[:, cols] = (
            value_part_ref[:, cols] + nn(key_ref[:, cols], state[rows, :])
        ).astype(BF16)


def layer_body(scale, own_ref, *refs):
    got_refs, gain_refs = refs[:PARTS], refs[PARTS:-2]
    out_ref, gain_grad_ref = refs[-2:]
    width = got_refs[0].shape[1]
    for i, got_ref in enumerate(got_refs):
        at = slice(i * width, (i + 1) * width)
        out_ref[:, at] = (own_ref[:, at] + got_ref[...].astype(F32)).astype(BF16)
    gain = gain_refs[0][...]
    if len(gain_refs) > 1:
        gain = gain + gain_refs[1][...]
    gain_grad_ref[...] = gain * scale


def on_device(queries, key_rows, value_rows, stretch_doc, head_gain, w_out, cotangent):
    tokens, width = queries.shape[1:]
    heads, dim = head_gain.shape
    model = w_out.shape[1]
    size = lax.axis_size("seq")
    matrix = 2 * tokens * dim * dim * heads
    square = 2 * tokens * tokens * dim * heads
    layer = tokens * width * model
    rows, summed, message = (tokens, width), (heads * dim, dim), (heads * dim + TAIL, dim)
    small, half = (heads, dim), (tokens // 2, model)
    distances = [1]
    while 2 * distances[-1] - 1 < size // 2 - 1:
        distances.append(2 * distances[-1])
    last = distances[-1]
    gains = size == 8

    beside = []

    def spread(outer, msg, forward):
        carry = gains and not forward
        if last == 2:
            pair = exchange(msg, blocks(size, 1, 0))
            far = exchange(msg, [(i, i + 3) for i in range(1, size - 3, 2)])
            if TIE[0] and forward or TIE[1] and not forward:
                pair, beside[0] = lax.optimization_barrier((pair, beside[0]))
            msg, *gain = call(
                functools.partial(pair_body, forward, carry), [(message, BF16)] + [(small, F32)] * carry, "vvvv",
                flops=0, moved=1 << 20,
            )(number, outer, msg, pair)
            even = odd = turned(msg, last if forward else -last)
            gain = [*gain, *(turned(block, -to) for block in gain for to in (size // 2, size // 2 + last))]
            even, far = lax.optimization_barrier((even, far))
            odd = even
            return [pair, far, even, odd], msg, gain
        terms = []
        for distance in distances[:-1]:
            even, odd = swaps(msg, distance)
            *terms, msg = call(
                functools.partial(merge_body, distance, forward, carry), [(summed, F32), (message, BF16)],
                "vvvvv" + "v" * len(terms), flops=0, moved=1 << 20,
            )(number, outer, msg, *terms, even, odd)
        return [*terms, *swaps(msg, last)], msg, []

    in_hbm = lambda block: pltpu.with_memory_space_constraint(block, pltpu.HBM)
    key, value, number, outer, msg = call(
        functools.partial(opening_body, heads, dim),
        [(rows, BF16)] * 2 + [((8, dim), F32), (summed, F32), (message, BF16)],
        "ahh", flops=matrix, moved=1 << 20, scratch=[pltpu.SMEM((1, 1), jnp.int32), pltpu.SemaphoreType.DMA((3,))],
    )(stretch_doc, in_hbm(key_rows[0]), in_hbm(value_rows[0]))
    query, w, weights, within, normed_grad = call(
        functools.partial(local_body, heads, dim),
        [(rows, BF16), ((width, model), BF16), ((heads * tokens, tokens), BF16), (rows, F32), (rows, F32)],
        "hvvhh", flops=2 * square + 2 * layer, moved=6 << 20,
        scratch=[pltpu.VMEM((tokens, model), BF16), pltpu.SemaphoreType.DMA((3,))],
    )(in_hbm(queries[0]), key, value, in_hbm(cotangent[0]), in_hbm(w_out))
    beside.append(within)
    sums, _, _ = spread(outer, msg, True)
    (within,) = beside
    state, keep, *send, grad, outer, msg, gain_part = call(
        functools.partial(forward_body, heads, dim, last),
        [
            (summed, BF16), ((tokens // 2, width), BF16), *[((tokens // 2, model // PARTS), BF16)] * PARTS,
            (rows, BF16), (summed, F32), (message, BF16), (small, F32),
        ],
        "vvvvvv" + "v" * len(sums), flops=2 * matrix + layer, moved=4 << 20, scratch=[pltpu.VMEM(rows, BF16)],
    )(number, query, within, normed_grad, head_gain, w, *sums)
    got = [lax.ppermute(part, "head", [(0, 1), (1, 0)]) for part in send]
    query_grad, key_part, value_part, own = call(
        functools.partial(backward_body, heads, dim),
        [(rows, BF16), (rows, F32), (rows, F32), (half, F32)],
        "vvvvvvvv", flops=0, moved=1 << 16,
    )(query, key, value, weights, grad, state, keep, w)
    beside[0] = key_part
    sums, msg, gain = spread(outer, msg, False)
    (key_part,) = beside
    scale = 1.0 / math.sqrt(size * lax.axis_size("dp") * tokens)
    if gains:
        (gain,) = call(gain_body, [(small, F32)], "vvvv", flops=0, moved=1 << 16)(*gain, sums[-2])
        gain = [gain, flipped(gain, 0, 1)]
    else:
        gain = [lax.psum(gain_part, ("seq", "dp"))]
    key_grad, value_grad = call(
        functools.partial(last_body, heads, dim, last), [(rows, BF16), (rows, BF16)],
        "vvvvv" + "v" * len(sums), flops=2 * matrix, moved=3 << 20,
    )(number, key, value, key_part, value_part, *sums)
    layer_out, gain_grad = call(
        functools.partial(layer_body, scale), [(half, BF16), (small, F32)], "v" + "v" * (PARTS + len(gain)),
        flops=0, moved=2 << 20,
    )(own, *got, *gain)
    return layer_out[None], query_grad[None], key_grad[None], value_grad[None], gain_grad


def solution(mesh):
    rows = P("dp", "seq", "head")
    return jax.shard_map(
        on_device,
        mesh=mesh,
        in_specs=(rows, rows, rows, P("dp", "seq"), P("head", None), P("head", None), P("dp", "seq", None)),
        out_specs=(P("dp", ("seq", "head"), None), rows, rows, rows, P("head", None)),
        check_vma=False,
    )
```

```python
import functools
import math

import jax
import jax.numpy as jnp
from jax import lax
from jax.experimental import pallas as pl
from jax.experimental.pallas import tpu as pltpu
from jax.sharding import PartitionSpec as P

EPSILON = 1e-05
F32 = jnp.float32
BF16 = jnp.bfloat16
TAIL = 16
GAIN = 4
PARTS = 1


def nn(a, b):
    return lax.dot_general(a, b, (((1,), (0,)), ((), ())), preferred_element_type=F32)


def nt(a, b):
    return lax.dot_general(a, b, (((1,), (1,)), ((), ())), preferred_element_type=F32)


def tn(a, b):
    return lax.dot_general(a, b, (((0,), (0,)), ((), ())), preferred_element_type=F32)


def call(body, outs, places, flops, moved, scratch=()):
    space = {"s": pltpu.SMEM, "v": pltpu.VMEM, "h": pltpu.HBM}
    return pl.pallas_call(
        body,
        out_shape=[jax.ShapeDtypeStruct(s, t) for s, t in outs],
        in_specs=[pl.BlockSpec(memory_space=space[p]) for p in places],
        out_specs=[pl.BlockSpec(memory_space=pltpu.VMEM) for _ in outs],
        scratch_shapes=list(scratch),
        name=getattr(body, "func", body).__name__,
        cost_estimate=pl.CostEstimate(flops=flops, bytes_accessed=moved, transcendentals=0),
        compiler_params=pltpu.CompilerParams(vmem_limit_bytes=40 << 20),
    )


def pairing(size, pairs):
    partner = {i: (j, False) for a, b in pairs for i, j in ((a, b), (b, a))}
    route = []
    for i in range(size):
        to, same_stretch = partner.get(i, (i, True))
        route += [(2 * i + core, 2 * to + (core ^ same_stretch)) for core in (0, 1)]
    return route


def exchange(block, pairs):
    return lax.ppermute(block, ("seq", "dp"), pairing(lax.axis_size("seq"), pairs))


def turning(size, loops):
    to = {a: b for loop in loops for a, b in zip(loop, loop[1:] + loop[:1])}
    return [
        (2 * i + core, 2 * to.get(i, i) + (core ^ (i not in to))) for i in range(size) for core in (0, 1)
    ]


def blocks(size, distance, odd):
    return [(i, i + distance) for i in range(size - distance) if (i // distance) % 2 == odd]


def swaps(block, distance):
    size = lax.axis_size("seq")
    return [exchange(block, blocks(size, distance, odd)) for odd in (0, 1)]


def turned(block, distance):
    size = lax.axis_size("seq")
    return lax.ppermute(block, "seq", [(i, (i + distance) % size) for i in range(size)])


def flipped(block, distance, cores):
    route = [
        (2 * i + core, 2 * (i ^ distance) + (core ^ cores))
        for i in range(lax.axis_size("seq"))
        for core in (0, 1)
    ]
    return lax.ppermute(block, ("seq", "dp"), route)


def put_tail(msg_ref, number, gain=None):
    rows, dim = msg_ref.shape[0] - TAIL, msg_ref.shape[1]
    high = jnp.zeros((GAIN, dim), F32) if gain is None else gain.astype(BF16).astype(F32)
    low = jnp.zeros((GAIN, dim), F32) if gain is None else gain - high
    low = low.astype(BF16).astype(F32)
    number = jnp.broadcast_to(number, (TAIL - 2 * GAIN, dim))
    msg_ref[rows:, :] = jnp.concatenate([high, low, number], axis=0).astype(BF16)
    return high + low


def sent_gain(msg_ref):
    tail = msg_ref[msg_ref.shape[0] - TAIL :, :].astype(F32)
    return tail[:GAIN, :] + tail[GAIN : 2 * GAIN, :]


def opened(msg):
    msg = msg.astype(F32)
    rows = msg.shape[0] - TAIL
    return msg[:rows, :], msg[rows + 2 * GAIN : rows + 2 * GAIN + 1, :]


def taken(even_ref, odd_ref, number, distance, forward):
    me, size = lax.axis_index("seq"), lax.axis_size("seq")
    upper = lax.rem(lax.div(me, distance), 2)
    from_odd = upper == 0 if forward else upper == 1
    there = me >= distance if forward else me + distance < size
    sums, theirs = opened(jnp.where(from_odd, odd_ref[...], even_ref[...]))
    return jnp.where(theirs == jnp.where(there, number, -1.0), sums, 0.0)


def beside(pair_ref, far_ref, number, forward):
    me, size = lax.axis_index("seq"), lax.axis_size("seq")
    in_pair = lax.rem(me, 2) == (1 if forward else 0)
    there = in_pair | (me >= 3 if forward else me + 3 < size)
    sums, theirs = opened(jnp.where(in_pair, pair_ref[...], far_ref[...]))
    return jnp.where(theirs == jnp.where(there, number, -1.0), sums, 0.0)


def total(refs, number, distance, forward):
    *near, even_ref, odd_ref = refs
    if len(near) == 1:
        first = near[0][...]
    else:
        first = beside(*near, number, forward)
    return first + taken(even_ref, odd_ref, number, distance, forward)


def opening_body(
    heads, dim, doc_ref, key_hbm, value_hbm,
    key_ref, value_ref, number_ref, sum_ref, msg_ref, sems,
):
    copies = [
        pltpu.make_async_copy(src, dst, sems.at[i])
        for i, (src, dst) in enumerate(((key_hbm, key_ref), (value_hbm, value_ref)))
    ]
    for copy in copies:
        copy.start()
    number = jnp.full(number_ref.shape, doc_ref[0, 0] + 1, jnp.int32).astype(F32)
    number_ref[...] = number
    put_tail(msg_ref, number[:1, :])
    copies[0].wait()
    copies[1].wait()
    for h in range(heads):
        cols, rows = slice(h * dim, (h + 1) * dim), slice(h * dim, (h + 1) * dim)
        sums = tn(key_ref[:, cols], value_ref[:, cols])
        sum_ref[rows, :] = sums
        msg_ref[rows, :] = sums.astype(BF16)


def local_body(
    heads, dim, query_hbm, key_ref, value_ref, cot_hbm, w_hbm,
    query_ref, w_ref, weight_ref, within_ref, normed_grad_ref, cot_ref, sems,
):
    copies = [
        pltpu.make_async_copy(src, dst, sems.at[i])
        for i, (src, dst) in enumerate(((query_hbm, query_ref), (cot_hbm, cot_ref), (w_hbm, w_ref)))
    ]
    for copy in copies:
        copy.start()
    tokens = query_ref.shape[0]
    causal = lax.broadcasted_iota(jnp.int32, (tokens, tokens), 0) >= lax.broadcasted_iota(
        jnp.int32, (tokens, tokens), 1
    )
    copies[0].wait()
    for h in range(heads):
        cols = slice(h * dim, (h + 1) * dim)
        scores = nt(query_ref[:, cols], key_ref[:, cols])
        weights = jnp.where(causal, scores, 0.0).astype(BF16)
        weight_ref[h * tokens : (h + 1) * tokens, :] = weights
        within_ref[:, cols] = nn(weights, value_ref[:, cols])
    copies[1].wait()
    copies[2].wait()
    normed_grad_ref[...] = nt(cot_ref[...], w_ref[...])


def merge_gain(gains, own_ref, other_ref):
    return sent_gain(own_ref) + sent_gain(other_ref) if gains else None


def pair_body(forward, gains, number_ref, sum_ref, own_ref, pair_ref, *refs):
    msg_ref, *gain_ref = refs
    rows = sum_ref.shape[0]
    number = number_ref[:1, :]
    leads = lax.rem(lax.axis_index("seq"), 2) == (1 if forward else 0)
    sums, theirs = opened(pair_ref[...])
    mine = sum_ref[...]
    same = theirs == number
    keep_mine, keep_theirs = same | leads, same | jnp.logical_not(leads)
    msg_ref[:rows, :] = (jnp.where(keep_mine, mine, 0.0) + jnp.where(keep_theirs, sums, 0.0)).astype(BF16)
    gain = put_tail(msg_ref, jnp.where(leads, number, theirs), merge_gain(gains, own_ref, pair_ref))
    if gains:
        gain_ref[0][...] = gain


def merge_body(distance, forward, gains, number_ref, sum_ref, own_ref, *refs):
    *term_ref, even_ref, odd_ref, out_ref, msg_ref = refs
    rows = sum_ref.shape[0]
    number = number_ref[:1, :]
    term = taken(even_ref, odd_ref, number, distance, forward)
    if term_ref:
        term = term + term_ref[0][...]
    out_ref[...] = term
    msg_ref[:rows, :] = (sum_ref[...] + term).astype(BF16)
    put_tail(msg_ref, number, merge_gain(gains, own_ref, even_ref))


def gain_body(own_ref, far_ref, farther_ref, near_ref, out_ref):
    out_ref[...] = (own_ref[...] + far_ref[...]) + (sent_gain(near_ref) + farther_ref[...])


def forward_body(
    heads, dim, distance, number_ref, query_ref, within_ref, normed_grad_ref, gain_ref, w_ref, *refs
):
    *sum_refs, state_ref, keep_ref = refs[: -5 - PARTS]
    send_refs = refs[-5 - PARTS : -5]
    grad_ref, outer_ref, msg_ref, gain_grad_ref, normed_ref = refs[-5:]
    half = keep_ref.shape[0]
    number = number_ref[:1, :]
    state_ref[...] = total(sum_refs, number, distance, True).astype(BF16)
    for h in range(heads):
        cols, rows = slice(h * dim, (h + 1) * dim), slice(h * dim, (h + 1) * dim)
        query = query_ref[:, cols]
        attended = within_ref[:, cols] + nn(query, state_ref[rows, :])
        inv_rms = lax.rsqrt(jnp.mean(attended * attended, axis=-1, keepdims=True) + EPSILON)
        unit = attended * inv_rms
        gain = gain_ref[h : h + 1, :]
        normed_ref[:, cols] = (unit * gain).astype(BF16)
        normed_grad = normed_grad_ref[:, cols]
        gain_grad_ref[h : h + 1, :] = jnp.sum(normed_grad * unit, axis=0, keepdims=True)
        scaled = normed_grad * gain
        grad = inv_rms * (scaled - unit * jnp.mean(scaled * unit, axis=-1, keepdims=True))
        grad = grad.astype(BF16)
        grad_ref[:, cols] = grad
        outer = tn(query, grad)
        outer_ref[rows, :] = outer
        msg_ref[rows, :] = outer.astype(BF16)
    gain_grad_ref[...] = put_tail(msg_ref, number, gain_grad_ref[...])
    head = lax.axis_index("head")
    keep_ref[...] = normed_ref[pl.ds(pl.multiple_of(head * half, half), half), :]
    give = normed_ref[pl.ds(pl.multiple_of((1 - head) * half, half), half), :]
    width = send_refs[0].shape[1]
    for i, send_ref in enumerate(send_refs):
        send_ref[...] = nn(give, w_ref[:, i * width : (i + 1) * width]).astype(BF16)


def backward_body(
    heads, dim, query_ref, key_ref, value_ref, weight_ref, grad_ref, state_ref, keep_ref, w_ref,
    query_grad_ref, key_part_ref, value_part_ref, own_ref,
):
    own_ref[...] = nn(keep_ref[...], w_ref[...])
    tokens = query_ref.shape[0]
    causal = lax.broadcasted_iota(jnp.int32, (tokens, tokens), 0) >= lax.broadcasted_iota(
        jnp.int32, (tokens, tokens), 1
    )
    for h in range(heads):
        cols, rows = slice(h * dim, (h + 1) * dim), slice(h * dim, (h + 1) * dim)
        grad = grad_ref[:, cols]
        grad_scores = nt(grad, value_ref[:, cols])
        grad_weights = jnp.where(causal, grad_scores, 0.0).astype(BF16)
        query_grad_ref[:, cols] = (
            nn(grad_weights, key_ref[:, cols]) + nt(grad, state_ref[rows, :])
        ).astype(BF16)
        key_part_ref[:, cols] = tn(grad_weights, query_ref[:, cols])
        value_part_ref[:, cols] = tn(weight_ref[h * tokens : (h + 1) * tokens, :], grad)


def last_body(
    heads, dim, distance, number_ref, key_ref, value_ref, key_part_ref, value_part_ref, *refs
):
    *sum_refs, key_grad_ref, value_grad_ref = refs
    state = total(sum_refs, number_ref[:1, :], distance, False).astype(BF16)
    for h in range(heads):
        cols, rows = slice(h * dim, (h + 1) * dim), slice(h * dim, (h + 1) * dim)
        key_grad_ref[:, cols] = (
            key_part_ref[:, cols] + nt(value_ref[:, cols], state[rows, :])
        ).astype(BF16)
        value_grad_ref[:, cols] = (
            value_part_ref[:, cols] + nn(key_ref[:, cols], state[rows, :])
        ).astype(BF16)


def layer_body(scale, own_ref, *refs):
    got_refs, gain_refs = refs[:PARTS], refs[PARTS:-2]
    out_ref, gain_grad_ref = refs[-2:]
    width = got_refs[0].shape[1]
    for i, got_ref in enumerate(got_refs):
        at = slice(i * width, (i + 1) * width)
        out_ref[:, at] = (own_ref[:, at] + got_ref[...].astype(F32)).astype(BF16)
    gain = gain_refs[0][...]
    if len(gain_refs) > 1:
        gain = gain + gain_refs[1][...]
    gain_grad_ref[...] = gain * scale


def on_device(queries, key_rows, value_rows, stretch_doc, head_gain, w_out, cotangent):
    tokens, width = queries.shape[1:]
    heads, dim = head_gain.shape
    model = w_out.shape[1]
    size = lax.axis_size("seq")
    matrix = 2 * tokens * dim * dim * heads
    square = 2 * tokens * tokens * dim * heads
    layer = tokens * width * model
    rows, summed, message = (tokens, width), (heads * dim, dim), (heads * dim + TAIL, dim)
    small, half = (heads, dim), (tokens // 2, model)
    distances = [1]
    while 2 * distances[-1] - 1 < size // 2 - 1:
        distances.append(2 * distances[-1])
    last = distances[-1]
    gains = size == 8

    beside = []

    def spread(outer, msg, forward):
        carry = gains and not forward
        if last == 2:
            pair = exchange(msg, blocks(size, 1, 0))
            loops = [[i, i + 3, i + 4] if forward else [i + 3, i, i - 1] for i in range(1, size - 3, 2)]
            far = lax.ppermute(msg, ("seq", "dp"), turning(size, loops))
            if not forward:
                pair, beside[0] = lax.optimization_barrier((pair, beside[0]))
            msg, *gain = call(
                functools.partial(pair_body, forward, carry), [(message, BF16)] + [(small, F32)] * carry, "vvvv",
                flops=0, moved=1 << 20,
            )(number, outer, msg, pair)
            even = odd = turned(msg, last if forward else -last)
            gain = [*gain, *(turned(block, -to) for block in gain for to in (size // 2, size // 2 + last))]
            even, far = lax.optimization_barrier((even, far))
            odd = even
            return [pair, far, even, odd], msg, gain
        terms = []
        for distance in distances[:-1]:
            even, odd = swaps(msg, distance)
            *terms, msg = call(
                functools.partial(merge_body, distance, forward, carry), [(summed, F32), (message, BF16)],
                "vvvvv" + "v" * len(terms), flops=0, moved=1 << 20,
            )(number, outer, msg, *terms, even, odd)
        return [*terms, *swaps(msg, last)], msg, []

    in_hbm = lambda block: pltpu.with_memory_space_constraint(block, pltpu.HBM)
    key, value, number, outer, msg = call(
        functools.partial(opening_body, heads, dim),
        [(rows, BF16)] * 2 + [((8, dim), F32), (summed, F32), (message, BF16)],
        "shh", flops=matrix, moved=1 << 20, scratch=[pltpu.SemaphoreType.DMA((2,))],
    )(stretch_doc, in_hbm(key_rows[0]), in_hbm(value_rows[0]))
    query, w, weights, within, normed_grad = call(
        functools.partial(local_body, heads, dim),
        [(rows, BF16), ((width, model), BF16), ((heads * tokens, tokens), BF16), (rows, F32), (rows, F32)],
        "hvvhh", flops=2 * square + 2 * layer, moved=6 << 20,
        scratch=[pltpu.VMEM((tokens, model), BF16), pltpu.SemaphoreType.DMA((3,))],
    )(in_hbm(queries[0]), key, value, in_hbm(cotangent[0]), in_hbm(w_out))
    beside.append(within)
    sums, _, _ = spread(outer, msg, True)
    (within,) = beside
    state, keep, *send, grad, outer, msg, gain_part = call(
        functools.partial(forward_body, heads, dim, last),
        [
            (summed, BF16), ((tokens // 2, width), BF16), *[((tokens // 2, model // PARTS), BF16)] * PARTS,
            (rows, BF16), (summed, F32), (message, BF16), (small, F32),
        ],
        "vvvvvv" + "v" * len(sums), flops=2 * matrix + layer, moved=4 << 20, scratch=[pltpu.VMEM(rows, BF16)],
    )(number, query, within, normed_grad, head_gain, w, *sums)
    got = [lax.ppermute(part, "head", [(0, 1), (1, 0)]) for part in send]
    query_grad, key_part, value_part, own = call(
        functools.partial(backward_body, heads, dim),
        [(rows, BF16), (rows, F32), (rows, F32), (half, F32)],
        "vvvvvvvv", flops=0, moved=1 << 16,
    )(query, key, value, weights, grad, state, keep, w)
    beside[0] = key_part
    sums, msg, gain = spread(outer, msg, False)
    (key_part,) = beside
    scale = 1.0 / math.sqrt(size * lax.axis_size("dp") * tokens)
    if gains:
        (gain,) = call(gain_body, [(small, F32)], "vvvv", flops=0, moved=1 << 16)(*gain, sums[-2])
        gain = [gain, flipped(gain, 0, 1)]
    else:
        gain = [lax.psum(gain_part, ("seq", "dp"))]
    key_grad, value_grad = call(
        functools.partial(last_body, heads, dim, last), [(rows, BF16), (rows, BF16)],
        "vvvvv" + "v" * len(sums), flops=2 * matrix, moved=3 << 20,
    )(number, key, value, key_part, value_part, *sums)
    layer_out, gain_grad = call(
        functools.partial(layer_body, scale), [(half, BF16), (small, F32)], "v" + "v" * (PARTS + len(gain)),
        flops=0, moved=2 << 20,
    )(own, *got, *gain)
    return layer_out[None], query_grad[None], key_grad[None], value_grad[None], gain_grad


def solution(mesh):
    rows = P("dp", "seq", "head")
    return jax.shard_map(
        on_device,
        mesh=mesh,
        in_specs=(rows, rows, rows, P("dp", "seq"), P("head", None), P("head", None), P("dp", "seq", None)),
        out_specs=(P("dp", ("seq", "head"), None), rows, rows, rows, P("head", None)),
        check_vma=False,
    )
```
